256 devices in a mesh: expert: 64 (over y, z, x_lo), pair: 4 (over x_hi, core).
Axes of the slice: x: 4 (x_hi: 2, x_lo: 2; x = x_hi * 2 + x_lo), y: 4, z: 8, core: 2. Of those that a mesh axis runs over, the one named last changes fastest.
Arguments:
- policy_tokens: bfloat16 [3072, 2048], P('expert'), may hold values from -6 to 6
- policy_cotangent: bfloat16 [3072, 2048], P('expert'), may hold values from -6 to 6
- frozen_tokens: bfloat16 [3072, 2048], P('expert'), may hold values from -6 to 6
- policy_route: int32 [3072, 8], P('expert'), may hold values from 0 to 127, all different within a row; in each aligned block of 48 rows (0 to 47, 48 to 95, ...) at most 4 rows name the same one
- policy_gates: float32 [3072, 8], P('expert'), may hold values from 0.1 to 1
- frozen_route: int32 [3072, 8], P('expert'), may hold values from 0 to 127, all different within a row; in each aligned block of 48 rows (0 to 47, 48 to 95, ...) at most 4 rows name the same one
- frozen_gates: float32 [3072, 8], P('expert'), may hold values from 0.1 to 1
- w_gate: bfloat16 [128, 2048, 768], P('expert', None, 'pair'), may hold values from -0.125 to 0.125
- w_up: bfloat16 [128, 2048, 768], P('expert', None, 'pair'), may hold values from -0.125 to 0.125
- w_down: bfloat16 [128, 768, 2048], P('expert', 'pair'), may hold values from -0.21875 to 0.21875
- adapter_down: bfloat16 [128, 768, 64], P('expert', 'pair'), may hold values from -0.21875 to 0.21875
- adapter_up: bfloat16 [128, 64, 2048], P('expert'), may hold values from -0.75 to 0.75
Outputs:
- frozen_out: bfloat16 [3072, 2048], P('expert', 'pair')
- input_grad: bfloat16 [3072, 2048], P('expert', 'pair')
- adapter_down_grad: float32 [128, 768, 64], P('expert', 'pair')
- adapter_up_grad: float32 [128, 64, 2048], P('expert')
The draws below stay inside these ranges and needn't reach their ends.
Inputs may be any that keep to these rules, and one draw needn't show every extreme that they name: `policy_route`: each row names 8 different experts; among the rows of one device no expert is named by more than 4 rows. `frozen_route`: each row names 8 different experts; among the rows of one device no expert is named by more than 4 rows.
All inputs are finite; a program needn't handle non-finite values.
Results may differ from the reference program's by a relative error of at most 0.012.
Values may be sent and summed in bfloat16 or wider, within the bound.
No kernel may reach another device: no remote copies, remote signals or barrier semaphores. Data moves between devices by JAX's collectives and lax.ppermute only.
A program may use at most 64 MiB of HBM per device.

```python
import math
from functools import partial
import jax
import jax.numpy as jnp
import numpy as np
from jax import lax

D = 2048
FF = 768
TOP = 8
RANK = 64
TOK_DEV = 48
EXPERTS = 128
SLOT = 4
TOKENS = 3072
N_EXPERT = 64
N_PAIR = 4


def shard_levels(stream_key, shape, shards, least, largest):
    gain, own = 1.0, jax.random.fold_in(stream_key, 6)
    for dim, shards_of in shards:
        draws = jnp.exp(jax.random.uniform(jax.random.fold_in(own, dim), (shards_of,), jnp.float32, least / len(shards), largest / len(shards)))
        gain = gain * jnp.repeat(draws, shape[dim] // shards_of).reshape([-1 if axis == dim else 1 for axis in range(len(shape))])
    return gain


def assign_block(rng, own, number, rows, count, top, bound, lean):
    ranking = jax.random.permutation(rng, count)
    packed, common = portions_of(count, rows * top, bound, lean, True), portions_of(count, rows * top, bound, lean, False)
    places = jnp.arange(count)

    def named(tallies, rotation):
        used = int((tallies > 0).sum())
        fixed = max(1, used // 4)
        shifted = fixed + (places - fixed + rotation * (used - fixed)) % max(1, count - fixed)
        return jnp.zeros((count,), jnp.int32).at[ranking[jnp.where(places < fixed, places, shifted)]].set(jnp.asarray(tallies, jnp.int32))

    tallies = jnp.where(number % 4 == 0, named(packed, number // 4), named(common, number - number // 4 - 1))
    mixed = jax.random.permutation(jax.random.fold_in(own, 3), count)
    giver, sink = mixed[0:count // 2 * 2:2], mixed[1:count // 2 * 2:2]
    slack = jnp.minimum(tallies[giver] - 1, bound - tallies[sink]) // 2
    slack = jnp.where((giver == ranking[0]) | (sink == ranking[0]) | (tallies[sink] == 0), 0, jnp.maximum(slack, 0))
    shifted = jax.random.randint(jax.random.fold_in(own, 4), (count // 2,), 0, 1 << 20) % (slack + 1)
    tallies = tallies.at[giver].add(-shifted).at[sink].add(shifted)
    labels = jnp.searchsorted(jnp.cumsum(tallies), jnp.arange(rows * top), side="right").astype(jnp.int32)
    table = labels.reshape(top, rows).T
    table = table[jax.random.permutation(jax.random.fold_in(own, 1), rows)]
    rotation = jax.random.randint(jax.random.fold_in(own, 2), (rows, 1), 0, top)
    return jnp.take_along_axis(table, (jnp.arange(top)[None, :] + rotation) % top, axis=1)


def portions_of(count, total, most, lean, full):
    portions = [(1 << 20) // math.isqrt(standing ** lean) + 1 for standing in range(1, count + 1)]
    largest = most if full else min(most, max(-(-total // count), total * portions[0] // sum(portions)))
    least = 1 if total - largest >= count - 1 else 0
    given, surplus = [largest] + [least] * (count - 1), total - largest - least * (count - 1)
    while surplus > 0:
        free = [i for i in range(1, count) if given[i] < largest] or [i for i in range(1, count) if given[i] < most]
        pool, budget = sum([portions[i] for i in free]), surplus
        for i in free:
            addition = min(most - given[i], max(1, budget * portions[i] // pool), surplus)
            given[i] = given[i] + addition
            surplus = surplus - addition
    return np.array(given)


def centred(rng, shape, scale, most, pieces=(), kind=jnp.bfloat16):
    gain = shard_levels(rng, shape, pieces, -0.22, 0.18) if pieces else 1.0
    drawn = jax.random.normal(rng, shape, jnp.float32) * scale * gain
    return jnp.minimum(jnp.maximum(drawn, -most), most).astype(kind)


def setup_inputs(seed: int = 0) -> dict:
    seeds = jax.random.split(jax.random.key(seed), 13)
    policy_tokens = centred(seeds[0], (TOKENS, D), 1.0, 6.0, ((0, 64),))
    policy_cotangent = centred(seeds[1], (TOKENS, D), 1.0, 6.0, ((0, 64),))
    frozen_tokens = centred(seeds[2], (TOKENS, D), 1.0, 6.0, ((0, 64),))
    policy_route_keys = jax.random.split(jax.random.fold_in(seeds[3], 1), TOKENS // TOK_DEV)
    policy_route_turns = jax.random.permutation(jax.random.fold_in(seeds[3], 3), TOKENS // TOK_DEV)
    policy_route = jax.vmap(lambda own, number: assign_block(jax.random.fold_in(seeds[3], 2), own, number, TOK_DEV, EXPERTS, TOP, SLOT, 2))(policy_route_keys, policy_route_turns).reshape((TOKENS, TOP))
    policy_gates = jnp.clip(0.1 + 0.9 * jax.random.uniform(seeds[4], (TOKENS, TOP), jnp.float32) ** shard_levels(seeds[4], (TOKENS, TOP), ((0, 64),), -0.2, 0.2), 0.1, 1.0)
    frozen_route_keys = jax.random.split(jax.random.fold_in(seeds[5], 1), TOKENS // TOK_DEV)
    frozen_route_turns = jax.random.permutation(jax.random.fold_in(seeds[5], 3), TOKENS // TOK_DEV)
    frozen_route = jax.vmap(lambda own, number: assign_block(jax.random.fold_in(seeds[5], 2), own, number, TOK_DEV, EXPERTS, TOP, SLOT, 2))(frozen_route_keys, frozen_route_turns).reshape((TOKENS, TOP))
    frozen_gates = jnp.clip(0.1 + 0.9 * jax.random.uniform(seeds[6], (TOKENS, TOP), jnp.float32) ** shard_levels(seeds[6], (TOKENS, TOP), ((0, 64),), -0.2, 0.2), 0.1, 1.0)
    w_gate = centred(seeds[7], (EXPERTS, D, FF), D ** -0.5, 0.125, ((0, 64), (2, 4)))
    w_up = centred(seeds[8], (EXPERTS, D, FF), D ** -0.5, 0.125, ((0, 64), (2, 4)))
    w_down = centred(seeds[9], (EXPERTS, FF, D), FF ** -0.5, 0.21875, ((0, 64), (1, 4)))
    adapter_down = centred(seeds[10], (EXPERTS, FF, RANK), FF ** -0.5, 0.21875, ((0, 64), (1, 4)))
    adapter_up = centred(seeds[11], (EXPERTS, RANK, D), RANK ** -0.5, 0.75, ((0, 64),))
    return dict(policy_tokens=policy_tokens, policy_cotangent=policy_cotangent, frozen_tokens=frozen_tokens, policy_route=policy_route, policy_gates=policy_gates, frozen_route=frozen_route, frozen_gates=frozen_gates, w_gate=w_gate, w_up=w_up, w_down=w_down, adapter_down=adapter_down, adapter_up=adapter_up)


adapter_scale = 2.0


def slot_tables(route, gates, experts, slot_count):
    chosen = route.reshape(-1).astype(jnp.int32)
    expert_ids = jnp.arange(experts, dtype=jnp.int32)
    one_hot = (chosen[:, None] == expert_ids[None, :]).astype(jnp.int32)
    earlier = jnp.cumsum(one_hot, axis=0).astype(jnp.int32) - one_hot
    position = jnp.sum(earlier * one_hot, axis=1).astype(jnp.int32)
    target = chosen * slot_count + position
    slot_ids = jnp.arange(experts * slot_count, dtype=jnp.int32)
    matched = (slot_ids[:, None] == target[None, :]).astype(jnp.float32)
    matched = matched.reshape(experts * slot_count, route.shape[0], route.shape[1])
    member_table = jnp.sum(matched, axis=2)
    gate_table = jnp.sum(matched * gates.astype(jnp.float32)[None, :, :], axis=2)
    return member_table, gate_table


def to_experts(sent):
    width = sent.shape[-1]
    grouped = sent.reshape(N_EXPERT, EXPERTS, SLOT, width).transpose(1, 0, 2, 3)
    return grouped.reshape(EXPERTS, N_EXPERT * SLOT, width)


def from_experts(rows):
    width = rows.shape[-1]
    grouped = rows.reshape(EXPERTS, N_EXPERT, SLOT, width).transpose(1, 0, 2, 3)
    return grouped.reshape(N_EXPERT, EXPERTS * SLOT, width)


def rounded_part(value):
    return lax.optimization_barrier(value.astype(jnp.bfloat16)).astype(jnp.float32)


def projections(rows, gate_weight, up_weight):
    gate_pre = jnp.dot(rows, gate_weight, preferred_element_type=jnp.float32)
    up_pre = jnp.dot(rows, up_weight, preferred_element_type=jnp.float32)
    sigmoid_gate = jax.nn.sigmoid(gate_pre)
    activated = gate_pre * sigmoid_gate
    hidden = (activated * up_pre).astype(jnp.bfloat16)
    return gate_pre, up_pre, sigmoid_gate, activated, hidden


def frozen_expert(operands):
    rows, gate_weight, up_weight, down_weight = operands
    gate_pre, up_pre, sigmoid_gate, activated, hidden = projections(rows, gate_weight, up_weight)
    group = FF // N_PAIR
    total = jnp.zeros((rows.shape[0], D), jnp.float32)
    for index in range(N_PAIR):
        lower = index * group
        piece = jnp.dot(hidden[:, lower:lower + group], down_weight[lower:lower + group, :], preferred_element_type=jnp.float32)
        total = total + rounded_part(piece)
    return total


def policy_expert(operands):
    rows, cot_rows, gate_weight, up_weight, down_weight, adapter_in, adapter_out = operands
    gate_pre, up_pre, sigmoid_gate, activated, hidden = projections(rows, gate_weight, up_weight)
    inner = jnp.dot(hidden, adapter_in, preferred_element_type=jnp.float32).astype(jnp.bfloat16)
    up_grad_adapter = adapter_scale * jnp.dot(inner.T, cot_rows, preferred_element_type=jnp.float32)
    inner_grad = (adapter_scale * jnp.dot(cot_rows, adapter_out.T, preferred_element_type=jnp.float32)).astype(jnp.bfloat16)
    down_grad_adapter = jnp.dot(hidden.T, inner_grad, preferred_element_type=jnp.float32)
    hidden_grad = jnp.dot(cot_rows, down_weight.T, preferred_element_type=jnp.float32)
    hidden_grad = hidden_grad + jnp.dot(inner_grad, adapter_in.T, preferred_element_type=jnp.float32)
    gate_grad = (hidden_grad * up_pre * sigmoid_gate * (1.0 + gate_pre * (1.0 - sigmoid_gate))).astype(jnp.bfloat16)
    up_grad = (hidden_grad * activated).astype(jnp.bfloat16)
    group = FF // N_PAIR
    row_grad = jnp.zeros((rows.shape[0], D), jnp.float32)
    for index in range(N_PAIR):
        lower = index * group
        piece = jnp.dot(gate_grad[:, lower:lower + group], gate_weight[:, lower:lower + group].T, preferred_element_type=jnp.float32)
        piece = piece + jnp.dot(up_grad[:, lower:lower + group], up_weight[:, lower:lower + group].T, preferred_element_type=jnp.float32)
        row_grad = row_grad + rounded_part(piece)
    return row_grad, down_grad_adapter, up_grad_adapter


def combine_rows(table, rows):
    summed = jnp.einsum("bst,bsd->btd", table, from_experts(rows), precision=lax.Precision.HIGHEST)
    return summed.reshape(TOKENS, rows.shape[-1]).astype(jnp.bfloat16)


def reference(policy_tokens, policy_cotangent, frozen_tokens, policy_route, policy_gates, frozen_route, frozen_gates, w_gate, w_up, w_down, adapter_down, adapter_up):
    tables = jax.vmap(partial(slot_tables, experts=EXPERTS, slot_count=SLOT))
    policy_member, policy_table = tables(policy_route.reshape(N_EXPERT, TOK_DEV, TOP), policy_gates.reshape(N_EXPERT, TOK_DEV, TOP))
    frozen_member, frozen_table = tables(frozen_route.reshape(N_EXPERT, TOK_DEV, TOP), frozen_gates.reshape(N_EXPERT, TOK_DEV, TOP))
    highest = lax.Precision.HIGHEST
    policy_blocks = policy_tokens.astype(jnp.float32).reshape(N_EXPERT, TOK_DEV, D)
    cot_blocks = policy_cotangent.astype(jnp.float32).reshape(N_EXPERT, TOK_DEV, D)
    frozen_blocks = frozen_tokens.astype(jnp.float32).reshape(N_EXPERT, TOK_DEV, D)
    policy_rows = to_experts(jnp.einsum("bst,btd->bsd", policy_member, policy_blocks, precision=highest).astype(jnp.bfloat16))
    cot_rows = to_experts(jnp.einsum("bst,btd->bsd", policy_table, cot_blocks, precision=highest).astype(jnp.bfloat16))
    frozen_rows = to_experts(jnp.einsum("bst,btd->bsd", frozen_member, frozen_blocks, precision=highest).astype(jnp.bfloat16))
    frozen_expert_out = lax.map(frozen_expert, (frozen_rows, w_gate, w_up, w_down))
    frozen_out = combine_rows(frozen_table, frozen_expert_out)
    row_grad, adapter_down_grad, adapter_up_grad = lax.map(policy_expert, (policy_rows, cot_rows, w_gate, w_up, w_down, adapter_down, adapter_up))
    input_grad = combine_rows(policy_member, row_grad)
    return frozen_out, input_grad, adapter_down_grad, adapter_up_grad
```

```python
import functools
import jax
import jax.numpy as jnp
from jax import lax
from jax.experimental import pallas as pl
from jax.experimental.pallas import tpu as pltpu
from jax.sharding import Mesh, PartitionSpec as P

BF = jnp.bfloat16
F32 = jnp.float32
SCALE = 2.0
SLOT = 4
PEERS = 32
TOK = 48
Q = 512


def nt(a, b):
    return lax.dot_general(a, b, (((1,), (1,)), ((), ())), preferred_element_type=F32)


def nn(a, b):
    return lax.dot_general(a, b, (((1,), (0,)), ((), ())), preferred_element_type=F32)


def tn(a, b):
    return lax.dot_general(a, b, (((0,), (0,)), ((), ())), preferred_element_type=F32)


def vmem_call(body, outs, args, flops=0, smem=1):
    specs = [pl.BlockSpec(memory_space=pltpu.SMEM)] * smem
    specs += [pl.BlockSpec(memory_space=pltpu.VMEM)] * (len(args) - smem)
    moved = sum(a.size * a.dtype.itemsize for a in args)
    moved += sum(o.size * o.dtype.itemsize for o in outs)
    return pl.pallas_call(
        body,
        out_shape=outs,
        in_specs=specs,
        out_specs=[pl.BlockSpec(memory_space=pltpu.VMEM)] * len(outs),
        compiler_params=pltpu.CompilerParams(vmem_limit_bytes=60 << 20),
        cost_estimate=pl.CostEstimate(flops=flops, bytes_accessed=moved, transcendentals=0),
    )(*args)


def tables(where_ref, meta, route_at, gate_at):
    rows = 2 * TOK
    cols = PEERS * 2 * SLOT
    col = lax.broadcasted_iota(jnp.int32, (rows, cols), 1)
    row = lax.broadcasted_iota(jnp.int32, (rows, cols), 0)
    expert = (4 * (col // 8) + where_ref[0]).astype(F32)
    named = jnp.zeros((rows, cols), F32)
    gate = jnp.zeros((rows, cols), F32)
    for k in range(8):
        match = meta[:, route_at + k : route_at + k + 1] == expert
        named = named + jnp.where(match, 1.0, 0.0)
        gate = gate + jnp.where(match, meta[:, gate_at + k : gate_at + k + 1], 0.0)
    r0 = lax.broadcasted_iota(jnp.int32, (rows, rows), 0)
    r1 = lax.broadcasted_iota(jnp.int32, (rows, rows), 1)
    earlier = jnp.where((r1 < r0) & ((r1 < TOK) == (r0 < TOK)), 1.0, 0.0)
    position = nn(earlier.astype(BF), named.astype(BF))
    here = (position == (col % SLOT).astype(F32)) & (((col // SLOT) % 2) == (row // TOK))
    member = jnp.where(here, named, 0.0)
    return member, jnp.where(here, gate, 0.0)


def pieces(x):
    hi = x.astype(BF)
    rest = x - hi.astype(F32)
    mid = rest.astype(BF)
    return hi, mid, (rest - mid.astype(F32)).astype(BF)


def select_body(where_ref, meta_a, meta_b, own, other, sent, member_p, gates_f):
    meta = jnp.concatenate([meta_a[...], meta_b[...]], axis=0)
    mem_p, gate_p = tables(where_ref, meta, 0, 8)
    mem_f, gate_f = tables(where_ref, meta, 16, 24)
    member_p[...] = mem_p.astype(BF)
    hi, mid, low = pieces(gate_f)
    gates_f[0] = hi
    gates_f[1] = mid
    gates_f[2] = low
    both = [jnp.concatenate([own[i], other[i]], axis=0) for i in range(3)]
    shape = (PEERS, 8, 2 * Q)
    sent[:, 0:8, :] = tn(mem_p.astype(BF), both[0]).astype(BF).reshape(shape)
    sent[:, 8:16, :] = tn(mem_f.astype(BF), both[1]).astype(BF).reshape(shape)
    hi, mid, low = pieces(gate_p)
    cot = tn(low, both[2]) + tn(mid, both[2]) + tn(hi, both[2])
    sent[:, 16:24, :] = cot.astype(BF).reshape(shape)


def main_body(
    where_ref, mine, theirs, wg, wu, wd, ad, au, wg2, wu2, wd2, ad2,
    grad_rows, frozen_rows, inner_part, down_grad, down_grad2,
):
    c, e = where_ref[1], where_ref[2]
    rows = PEERS * 8

    def block(ref, i, h):
        return ref[:, 8 * i : 8 * i + 8, h * Q : (h + 1) * Q].reshape(rows, Q)

    def contract(i, weight, index):
        total = None
        for ref, core in ((mine, c), (theirs, 1 - c)):
            for h in range(2):
                at = pl.ds(pl.multiple_of((2 * h + core) * Q, Q), Q)
                w = weight[:, at] if index is None else weight[index, :, at]
                part = nt(block(ref, i, h), w)
                total = part if total is None else total + part
        return total

    inner_grad = (SCALE * contract(2, au, e)).astype(BF)
    inner = None
    grads, frozen = [], []
    for n, (g, u, d, a, index) in enumerate(((wg, wu, wd, ad, e), (wg2, wu2, wd2, ad2, None))):
        gate_pre = contract(1, g, index)
        up_pre = contract(1, u, index)
        frozen.append((gate_pre * jax.nn.sigmoid(gate_pre) * up_pre).astype(BF))
        gate_pre = contract(0, g, index)
        up_pre = contract(0, u, index)
        sigmoid = jax.nn.sigmoid(gate_pre)
        activated = gate_pre * sigmoid
        hidden = (activated * up_pre).astype(BF)
        adapter = a[...] if index is None else a[index]
        part = nt(hidden, adapter)
        inner = part if inner is None else inner + part
        out = down_grad if n == 0 else down_grad2
        out[...] = tn(inner_grad, hidden)
        hidden_grad = contract(2, d, index) + nn(inner_grad, adapter)
        gate_grad = (hidden_grad * up_pre * sigmoid * (1.0 + gate_pre * (1.0 - sigmoid))).astype(BF)
        grads.append((gate_grad, (hidden_grad * activated).astype(BF)))
    inner_part[...] = inner

    def take(weight, index, at):
        return weight[:, at] if index is None else weight[index, :, at]

    for q in range(4):
        at = slice(q * Q, (q + 1) * Q)
        frozen_rows[:, at] = (
            nn(frozen[0], take(wd, e, at)) + nn(frozen[1], take(wd2, None, at))
        ).astype(BF)
        total = nn(grads[0][0], take(wg, e, at)) + nn(grads[0][1], take(wu, e, at))
        total = total + nn(grads[1][0], take(wg2, None, at)) + nn(grads[1][1], take(wu2, None, at))
        grad_rows[:, at] = total.astype(BF)


def combine_body(member_p, gates_f, back, out):
    rows = PEERS * 8
    out[0] = (
        nn(gates_f[2], back[:, 8:16, :].reshape(rows, 2 * Q))
        + nn(gates_f[1], back[:, 8:16, :].reshape(rows, 2 * Q))
        + nn(gates_f[0], back[:, 8:16, :].reshape(rows, 2 * Q))
    )
    out[1] = nn(member_p[...], back[:, 0:8, :].reshape(rows, 2 * Q))


def swap(x, axis):
    return lax.ppermute(x, axis, [(0, 1), (1, 0)])


def swap_both(x):
    return lax.ppermute(x, ("xl", "xh"), [(i, 3 - i) for i in range(4)])


def exchange(x):
    return lax.all_to_all(x, ("y", "z"), split_axis=0, concat_axis=0, tiled=True)


def pick(c, a, b):
    return jnp.where(c == 0, a, b)


def per_device(
    policy_tokens, policy_cotangent, frozen_tokens, policy_route, policy_gates,
    frozen_route, frozen_gates, w_gate, w_up, w_down, adapter_down, adapter_up,
):
    c, xh, xl = lax.axis_index("core"), lax.axis_index("xh"), lax.axis_index("xl")
    where = jnp.stack([2 * xl + xh, c, xh]).astype(jnp.int32)
    wg, wu = w_gate.swapaxes(1, 2), w_up.swapaxes(1, 2)
    ad = adapter_down.swapaxes(1, 2)

    def away(w):
        return lax.dynamic_index_in_dim(w, 1 - xh, 0, keepdims=False)

    def half(x):
        return jnp.concatenate(
            [pick(c, x[:, 0:Q], x[:, Q : 2 * Q]), pick(c, x[:, 2 * Q : 3 * Q], x[:, 3 * Q :])], axis=1
        )

    meta = jnp.concatenate(
        [policy_route.astype(F32), policy_gates, frozen_route.astype(F32), frozen_gates], axis=1
    )
    own = jnp.stack([half(policy_tokens), half(frozen_tokens), half(policy_cotangent)])
    meta_b, other = swap(meta, "xl"), swap(own, "xl")
    wg2, wu2, wd2, ad2 = [swap(away(w), "xh") for w in (wg, wu, w_down, ad)]

    sent, member_p, gates_f = vmem_call(
        select_body,
        [
            jax.ShapeDtypeStruct((PEERS, 24, 2 * Q), BF),
            jax.ShapeDtypeStruct((2 * TOK, 256), BF),
            jax.ShapeDtypeStruct((3, 2 * TOK, 256), BF),
        ],
        [where, meta, meta_b, own, other],
        flops=10**9,
    )
    mine = exchange(sent)
    theirs = swap(mine, "core")
    rows = PEERS * 8
    grad_rows, frozen_rows, inner_part, down_grad, down_grad2 = vmem_call(
        main_body,
        [
            jax.ShapeDtypeStruct((rows, 4 * Q), BF),
            jax.ShapeDtypeStruct((rows, 4 * Q), BF),
            jax.ShapeDtypeStruct((rows, 64), F32),
            jax.ShapeDtypeStruct((64, 192), F32),
            jax.ShapeDtypeStruct((64, 192), F32),
        ],
        [where, mine, theirs, wg, wu, w_down, ad, adapter_up, wg2, wu2, wd2, ad2],
        flops=4 * 10**9,
    )

    def half_rows(x, core):
        return jnp.concatenate(
            [pick(core, x[:, 0:Q], x[:, Q : 2 * Q]), pick(core, x[:, 2 * Q : 3 * Q], x[:, 3 * Q :])], axis=1
        ).reshape(PEERS, 8, 2 * Q)

    give = jnp.concatenate([half_rows(grad_rows, 1 - c), half_rows(frozen_rows, 1 - c)], axis=1)
    keep = jnp.concatenate([half_rows(grad_rows, c), half_rows(frozen_rows, c)], axis=1)
    got = swap(give, "core")
    total = (keep.astype(F32) + got.astype(F32)).astype(BF)
    back = exchange(total)
    (both,) = vmem_call(
        combine_body,
        [jax.ShapeDtypeStruct((2, 2 * TOK, 2 * Q), F32)],
        [member_p, gates_f, back],
        flops=10**8,
        smem=0,
    )

    def part(j, h):
        return both[:, j * TOK : (j + 1) * TOK, h * Q : (h + 1) * Q]

    def quarter(j, h):
        return pick(h, part(j, 0), part(j, 1))

    outs = quarter(0, xh) + swap(quarter(0, 1 - xh), "xh")
    outs = outs + swap(quarter(1, xh), "xl") + swap_both(quarter(1, 1 - xh))
    outs = outs.astype(BF)

    inner = (inner_part + swap(inner_part, "core")).astype(BF)
    cot = mine[:, 16:24, :].reshape(rows, 2 * Q)
    up_half = SCALE * tn(inner, cot)
    up_other = swap(up_half, "core")
    lo, hi = pick(c, up_half, up_other), pick(c, up_other, up_half)
    up_own = jnp.concatenate([lo[:, :Q], hi[:, :Q], lo[:, Q:], hi[:, Q:]], axis=1)
    up_away = swap(up_own, "xh")
    up_grad = jnp.stack([pick(xh, up_own, up_away), pick(xh, up_away, up_own)])
    down_away = swap(down_grad2, "xh")
    down = jnp.stack([pick(xh, down_grad, down_away), pick(xh, down_away, down_grad)]).swapaxes(1, 2)
    return outs[0], outs[1], down, up_grad


def solution(mesh):
    fine = Mesh(mesh.devices.reshape(4, 8, 2, 2, 2), ("y", "z", "xl", "xh", "core"))
    ex, pr = ("y", "z", "xl"), ("xh", "core")
    in_specs = (P(ex, None),) * 7 + (
        P(ex, None, pr), P(ex, None, pr), P(ex, pr, None), P(ex, pr, None), P(ex, None, None),
    )
    out_specs = (P(ex, pr), P(ex, pr), P(ex, pr, None), P(ex, None, None))
    return jax.shard_map(
        per_device, mesh=fine, in_specs=in_specs, out_specs=out_specs, check_vma=False
    )
```

```python
import jax
import jax.numpy as jnp
from jax import lax
from jax.experimental import pallas as pl
from jax.experimental.pallas import tpu as pltpu
from jax.sharding import Mesh, PartitionSpec as P

BF = jnp.bfloat16
F32 = jnp.float32
SCALE = 2.0
SLOT = 4
PEERS = 32
TOK = 48
Q = 512
ROWS = 256
FULL = 67043328


def nt(a, b):
    return lax.dot_general(a, b, (((1,), (1,)), ((), ())), preferred_element_type=F32)


def nn(a, b):
    return lax.dot_general(a, b, (((1,), (0,)), ((), ())), preferred_element_type=F32)


def tn(a, b):
    return lax.dot_general(a, b, (((0,), (0,)), ((), ())), preferred_element_type=F32)


def vmem_call(body, outs, args, flops=0, mib=16):
    specs = [pl.BlockSpec(memory_space=pltpu.SMEM)]
    specs += [pl.BlockSpec(memory_space=pltpu.VMEM)] * (len(args) - 1)
    moved = sum(a.size * a.dtype.itemsize for a in args)
    moved += sum(o.size * o.dtype.itemsize for o in outs)
    return pl.pallas_call(
        body,
        out_shape=outs,
        in_specs=specs,
        out_specs=[pl.BlockSpec(memory_space=pltpu.VMEM)] * len(outs),
        compiler_params=pltpu.CompilerParams(vmem_limit_bytes=mib << 20),
        cost_estimate=pl.CostEstimate(flops=flops, bytes_accessed=moved, transcendentals=0),
    )(*args)


def sds(shape, dtype):
    return jax.ShapeDtypeStruct(shape, dtype)


def quarter(h, core):
    return pl.ds(pl.multiple_of((2 * h + core) * Q, Q), Q)


def halves_body(where_ref, policy, frozen, cotangent, own, sems):
    copies = []
    for n, ref in enumerate((policy, frozen, cotangent)):
        for h in range(2):
            copies.append(pltpu.make_async_copy(
                ref.at[:, quarter(h, where_ref[1])], own.at[n, :, h * Q : (h + 1) * Q], sems.at[n, h]
            ))
    for copy in copies:
        copy.start()
    for copy in copies:
        copy.wait()


def bundle_body(where_ref, wg, wu, wd, out, sems):
    away = 1 - where_ref[2]
    copies = [
        pltpu.make_async_copy(ref.at[away], out.at[n], sems.at[n]) for n, ref in enumerate((wg, wu, wd))
    ]
    for copy in copies:
        copy.start()
    for copy in copies:
        copy.wait()


def tables(where_ref, meta_a, meta_b, at):
    cols = 2 * TOK
    meta = jnp.concatenate([meta_a[at : at + 16], meta_b[at : at + 16]], axis=1)
    col = lax.broadcasted_iota(jnp.int32, (ROWS, cols), 1)
    row = lax.broadcasted_iota(jnp.int32, (ROWS, cols), 0)
    expert = (4 * (row // 8) + where_ref[0]).astype(F32)
    named = jnp.zeros((ROWS, cols), F32)
    gate = jnp.zeros((ROWS, cols), F32)
    for k in range(8):
        match = meta[k : k + 1] == expert
        named = named + jnp.where(match, 1.0, 0.0)
        gate = gate + jnp.where(match, meta[8 + k : 9 + k], 0.0)
    r0 = lax.broadcasted_iota(jnp.int32, (cols, cols), 0)
    r1 = lax.broadcasted_iota(jnp.int32, (cols, cols), 1)
    earlier = jnp.where((r0 < r1) & ((r0 < TOK) == (r1 < TOK)), 1.0, 0.0)
    position = nn(named.astype(BF), earlier.astype(BF))
    here = (position == (row % SLOT).astype(F32)) & (((row // SLOT) % 2 == 1) == (col >= TOK))
    return jnp.where(here, named, 0.0), jnp.where(here, gate, 0.0)


def pieces(x):
    hi = x.astype(BF)
    rest = x - hi.astype(F32)
    mid = rest.astype(BF)
    return hi, mid, (rest - mid.astype(F32)).astype(BF)


def select_body(where_ref, meta_a, meta_b, own, other, sent, both, sems):
    copies = [
        pltpu.make_async_copy(ref, both.at[:, TOK * n : TOK * n + TOK, :], sems.at[n])
        for n, ref in enumerate((own, other))
    ]
    for copy in copies:
        copy.start()
    member_p, gate_p = tables(where_ref, meta_a, meta_b, 0)
    member_f, _ = tables(where_ref, meta_a, meta_b, 16)
    for copy in copies:
        copy.wait()
    for i, member in enumerate((member_p, member_f, member_p)):
        picked = nn(member.astype(BF), both[i])
        if i == 2:
            picked = picked * jnp.sum(gate_p, axis=1, keepdims=True)
        sent[:, 8 * i : 8 * i + 8, :] = picked.astype(BF).reshape(PEERS, 8, 2 * Q)


def home_body(where_ref, meta_a, meta_b, member_p, gates_f):
    member, _ = tables(where_ref, meta_a, meta_b, 0)
    member_p[...] = member.T.astype(BF)
    _, gate = tables(where_ref, meta_a, meta_b, 16)
    hi, mid, low = pieces(gate.T)
    gates_f[0] = hi
    gates_f[1] = mid
    gates_f[2] = low


def contract(where_ref, mine, theirs, i, weight, index):
    total = None
    for ref, core in ((mine, where_ref[1]), (theirs, 1 - where_ref[1])):
        for h in range(2):
            x = ref[:, 8 * i : 8 * i + 8, h * Q : (h + 1) * Q].reshape(ROWS, Q)
            at = quarter(h, core)
            part = nt(x, weight[:, at] if index is None else weight[index, :, at])
            total = part if total is None else total + part
    return total


def main_body(
    where_ref, mine, theirs, wg, wu, wd, ad, au, w2, ad2, give, keep, inner, down_grad, down_grad2
):
    e = where_ref[2]
    weights = ((wg.at[e], wu.at[e], wd.at[e]), (w2.at[0], w2.at[1], w2.at[2]))
    adapters = (ad[e], ad2[...])

    def dot(i, weight):
        return contract(where_ref, mine, theirs, i, weight, None)

    def expand(pairs, i):
        for out, core in ((give, 1 - where_ref[1]), (keep, where_ref[1])):
            for h in range(2):
                at = quarter(h, core)
                total = None
                for x, w in pairs:
                    part = nn(x, w[:, at])
                    total = part if total is None else total + part
                out[:, 8 * i : 8 * i + 8, h * Q : (h + 1) * Q] = total.astype(BF).reshape(PEERS, 8, Q)

    pairs = []
    for g, u, d in weights:
        gate_pre = dot(1, g)
        pairs.append(((gate_pre * jax.nn.sigmoid(gate_pre) * dot(1, u)).astype(BF), d))
    expand(pairs, 1)
    inner_grad = (SCALE * dot(2, au.at[e])).astype(BF)
    pairs = []
    total = None
    for n, (g, u, d) in enumerate(weights):
        gate_pre = dot(0, g)
        up_pre = dot(0, u)
        sigmoid = jax.nn.sigmoid(gate_pre)
        activated = gate_pre * sigmoid
        hidden = (activated * up_pre).astype(BF)
        part = nt(hidden, adapters[n])
        total = part if total is None else total + part
        (down_grad, down_grad2)[n][...] = tn(inner_grad, hidden)
        hidden_grad = dot(2, d) + nn(inner_grad, adapters[n])
        slope = up_pre * sigmoid * (1.0 + gate_pre * (1.0 - sigmoid))
        pairs.append(((hidden_grad * slope).astype(BF), g))
        pairs.append(((hidden_grad * activated).astype(BF), u))
    inner[...] = total
    expand(pairs, 0)


def up_body(where_ref, inner_a, inner_b, cot, out):
    inner = (inner_a[...] + inner_b[...]).astype(BF)
    out[...] = SCALE * tn(inner, cot[:, 16:24, :].reshape(ROWS, 2 * Q))


def combine_body(where_ref, member, gates, back, own, to_xh, to_xl, to_both):
    for at, near, far in ((where_ref[2], own, to_xl), (1 - where_ref[2], to_xh, to_both)):
        lanes = pl.ds(pl.multiple_of(at * Q, Q), Q)
        grads = back[:, 0:8, lanes].reshape(ROWS, Q)
        frozen = back[:, 8:16, lanes].reshape(ROWS, Q)
        frozen = nn(gates[2], frozen) + nn(gates[1], frozen) + nn(gates[0], frozen)
        grads = nn(member[...], grads)
        for n, total in enumerate((frozen, grads)):
            near[n] = total[:TOK].astype(near.dtype)
            far[n] = total[TOK:].astype(far.dtype)


def swap(x, axis):
    return lax.ppermute(x, axis, [(0, 1), (1, 0)])


def swap_both(x):
    return lax.ppermute(x, ("xl", "xh"), [(i, 3 - i) for i in range(4)])


def exchange(x):
    return lax.all_to_all(x, ("y", "z"), split_axis=0, concat_axis=0, tiled=True)


def pick(c, a, b):
    return jnp.where(c == 0, a, b)


def step(
    policy_tokens, policy_cotangent, frozen_tokens, policy_route, policy_gates,
    frozen_route, frozen_gates, w_gate, w_up, w_down, adapter_down, adapter_up,
):
    c, xh, xl = lax.axis_index("core"), lax.axis_index("xh"), lax.axis_index("xl")
    where = jnp.stack([2 * xl + xh, c, xh]).astype(jnp.int32)
    wg, wu = w_gate.swapaxes(1, 2), w_up.swapaxes(1, 2)
    ad = adapter_down.swapaxes(1, 2)

    def away(w):
        return lax.dynamic_index_in_dim(w, 1 - xh, 0, keepdims=False)

    meta = jnp.concatenate(
        [policy_route.T.astype(F32), policy_gates.T, frozen_route.T.astype(F32), frozen_gates.T]
    )
    hbm = pl.BlockSpec(memory_space=pltpu.HBM)
    own = pl.pallas_call(
        halves_body,
        name="halves",
        out_shape=sds((3, TOK, 2 * Q), BF),
        in_specs=[pl.BlockSpec(memory_space=pltpu.SMEM), hbm, hbm, hbm],
        out_specs=pl.BlockSpec(memory_space=pltpu.VMEM),
        scratch_shapes=[pltpu.SemaphoreType.DMA((3, 2))],
        compiler_params=pltpu.CompilerParams(vmem_limit_bytes=FULL),
    )(where, policy_tokens, frozen_tokens, policy_cotangent)
    other = swap(own, "xl")
    meta_b = swap(meta, "xl")
    mine_w = pl.pallas_call(
        bundle_body,
        name="bundle",
        out_shape=sds((3, 192, 4 * Q), BF),
        in_specs=[pl.BlockSpec(memory_space=pltpu.SMEM), hbm, hbm, hbm],
        out_specs=pl.BlockSpec(memory_space=pltpu.VMEM),
        scratch_shapes=[pltpu.SemaphoreType.DMA((3,))],
        compiler_params=pltpu.CompilerParams(vmem_limit_bytes=FULL),
    )(where, wg, wu, w_down)
    w2 = swap(mine_w, "xh")
    ad2 = swap(away(ad), "xh")

    vmem = pl.BlockSpec(memory_space=pltpu.VMEM)
    sent = pl.pallas_call(
        select_body,
        name="select",
        out_shape=sds((PEERS, 24, 2 * Q), BF),
        in_specs=[pl.BlockSpec(memory_space=pltpu.SMEM), vmem, vmem, hbm, hbm],
        out_specs=vmem,
        scratch_shapes=[pltpu.VMEM((3, 2 * TOK, 2 * Q), BF), pltpu.SemaphoreType.DMA((2,))],
        compiler_params=pltpu.CompilerParams(vmem_limit_bytes=FULL),
    )(where, meta, meta_b, own, other)
    member_p, gates_f = vmem_call(
        home_body, [sds((2 * TOK, ROWS), BF), sds((3, 2 * TOK, ROWS), BF)],
        [where, meta, meta_b], flops=10**8, mib=8,
    )
    mine = exchange(sent)
    theirs = swap(mine, "core")
    wide = sds((PEERS, 16, 2 * Q), BF)
    give, keep, inner, down_grad, down_grad2 = vmem_call(
        main_body,
        [wide, wide, sds((ROWS, 64), F32), sds((64, 192), F32), sds((64, 192), F32)],
        [where, mine, theirs, wg, wu, w_down, ad, adapter_up, w2, ad2], flops=4 * 10**9, mib=28,
    )
    total = (keep.astype(F32) + swap(give, "core").astype(F32)).astype(BF)
    back = exchange(total)
    own, to_xh, to_xl, to_both = vmem_call(
        combine_body, [sds((2, TOK, Q), F32)] + [sds((2, TOK, Q), BF)] * 3,
        [where, member_p, gates_f, back], flops=10**8, mib=8,
    )
    from_xh = swap(to_xh, "xh")
    from_xl = swap(to_xl, "xl")
    from_both = swap_both(to_both)
    outs = own + from_xh.astype(F32) + from_xl.astype(F32) + from_both.astype(F32)
    frozen_out, input_grad = outs[0].astype(BF), outs[1].astype(BF)

    (up_half,) = vmem_call(
        up_body, [sds((64, 2 * Q), F32)], [where, inner, swap(inner, "core"), mine],
        flops=10**8, mib=6,
    )
    up_other = swap(up_half, "core")
    lo, hi = pick(c, up_half, up_other), pick(c, up_other, up_half)
    up_own = jnp.concatenate([lo[:, :Q], hi[:, :Q], lo[:, Q:], hi[:, Q:]], axis=1)
    up_away = swap(up_own, "xh")
    up_grad = jnp.stack([pick(xh, up_own, up_away), pick(xh, up_away, up_own)])
    down_away = swap(down_grad2, "xh")
    down = jnp.stack([pick(xh, down_grad, down_away), pick(xh, down_away, down_grad)]).swapaxes(1, 2)
    return frozen_out, input_grad, down, up_grad


def solution(mesh):
    fine = Mesh(mesh.devices.reshape(4, 8, 2, 2, 2), ("y", "z", "xl", "xh", "core"))
    ex, pr = ("y", "z", "xl"), ("xh", "core")
    in_specs = (P(ex, None),) * 7 + (
        P(ex, None, pr), P(ex, None, pr), P(ex, pr, None), P(ex, pr, None), P(ex, None, None),
    )
    out_specs = (P(ex, pr), P(ex, pr), P(ex, pr, None), P(ex, None, None))
    return jax.shard_map(step, mesh=fine, in_specs=in_specs, out_specs=out_specs, check_vma=False)
```

```python
import jax
import jax.numpy as jnp
from jax import lax
from jax.experimental import pallas as pl
from jax.experimental.pallas import tpu as pltpu
from jax.sharding import Mesh, PartitionSpec as P

BF = jnp.bfloat16
F32 = jnp.float32
SCALE = 2.0
SLOT = 4
PEERS = 32
TOK = 48
Q = 512
ROWS = 256
META = 3 * TOK
FULL = 67043328


def nt(a, b):
    return lax.dot_general(a, b, (((1,), (1,)), ((), ())), preferred_element_type=F32)


def nn(a, b):
    return lax.dot_general(a, b, (((1,), (0,)), ((), ())), preferred_element_type=F32)


def tn(a, b):
    return lax.dot_general(a, b, (((0,), (0,)), ((), ())), preferred_element_type=F32)


def vmem_call(body, outs, args, flops=10**8, mib=16):
    return kernel(body, outs, args, [], "v" * len(args), "v" * len(outs), flops, mib << 20)


SPACES = {
    "h": pl.BlockSpec(memory_space=pltpu.HBM),
    "v": pl.BlockSpec(memory_space=pltpu.VMEM),
}


def kernel(body, outs, args, scratch, ins, places, flops=10**8, limit=FULL):
    moved = sum(a.size * a.dtype.itemsize for a in [*args, *outs])

    def run(*refs):
        xl, xh = lax.axis_index("xl"), lax.axis_index("xh")
        body((2 * xl + xh, lax.axis_index("core"), xh), *refs)

    return pl.pallas_call(
        run,
        out_shape=outs,
        in_specs=[SPACES[x] for x in ins],
        out_specs=[SPACES[x] for x in places],
        scratch_shapes=scratch,
        compiler_params=pltpu.CompilerParams(vmem_limit_bytes=limit),
        cost_estimate=pl.CostEstimate(flops=flops, bytes_accessed=moved, transcendentals=0),
    )(*args)


def sds(shape, dtype):
    return jax.ShapeDtypeStruct(shape, dtype)


def quarter(h, core):
    return pl.ds(pl.multiple_of((2 * h + core) * Q, Q), Q)


def pieces(x):
    hi = x.astype(BF)
    rest = x - hi.astype(F32)
    mid = rest.astype(BF)
    return hi, mid, (rest - mid.astype(F32)).astype(BF)


def run_all(copies):
    for copy in copies:
        copy.start()
    for copy in copies:
        copy.wait()


def halves_body(where, policy, frozen, cotangent, route_p, gates_p, route_f, gates_f, own, sems):
    copies = []
    for n, ref in enumerate((policy, frozen, cotangent)):
        for h in range(2):
            copies.append(pltpu.make_async_copy(
                ref.at[:, quarter(h, where[1])],
                own.at[TOK * n : TOK * n + TOK, h * Q : (h + 1) * Q],
                sems.at[n, h],
            ))
    for copy in copies:
        copy.start()
    pad = jnp.zeros((8, 128 - TOK), BF)
    for n, (route, gates) in enumerate(((route_p, gates_p), (route_f, gates_f))):
        for p, x in enumerate((route[...].astype(F32).astype(BF), *pieces(gates[...]))):
            at = 128 * (4 * n + p)
            own[META:, at : at + 128] = jnp.concatenate([x, pad], axis=1)
    for copy in copies:
        copy.wait()


def bundle_body(where, wg, wu, wd, ad, out, stage, small, sems):
    away = 1 - where[2]
    last = pltpu.make_async_copy(ad.at[away], small, sems.at[0, 12])
    into, back = [], []
    for n, ref in enumerate((wg, wu, wd)):
        for k in range(4):
            at = 192 * n + 48 * k
            piece = stage.at[at : at + 48, :]
            src = ref.at[away, 48 * k : 48 * k + 48, :]
            into.append(pltpu.make_async_copy(src, piece, sems.at[0, 4 * n + k]))
            back.append(pltpu.make_async_copy(piece, out.at[at : at + 48, :], sems.at[1, 4 * n + k]))
    for copy in (*into, last):
        copy.start()
    for a, b in zip(into, back):
        a.wait()
        b.start()
    last.wait()
    pad = jnp.zeros((8, 64), BF)
    rest = [jnp.concatenate([small[8 * k : 8 * k + 8, :], pad], axis=1) for k in range(8)]
    stage[576:584, :] = jnp.concatenate(rest, axis=1)
    tail = pltpu.make_async_copy(stage.at[576:584, :], out.at[576:584, :], sems.at[1, 12])
    tail.start()
    for copy in (*back, tail):
        copy.wait()


def blocks(meta_a, meta_b, n):
    out = []
    for meta in (meta_a, meta_b):
        part = [meta[:, 128 * (4 * n + p) : 128 * (4 * n + p) + TOK].astype(F32) for p in range(4)]
        out.append((part[0], part[1] + part[2] + part[3]))
    return [jnp.concatenate([a, b], axis=1) for a, b in zip(*out)]


def tables(where, meta_a, meta_b, n):
    cols = 2 * TOK
    route, gates = blocks(meta_a, meta_b, n)
    col = lax.broadcasted_iota(jnp.int32, (ROWS, cols), 1)
    row = lax.broadcasted_iota(jnp.int32, (ROWS, cols), 0)
    expert = (4 * (row // 8) + where[0]).astype(F32)
    named = jnp.zeros((ROWS, cols), F32)
    gate = jnp.zeros((ROWS, cols), F32)
    for k in range(8):
        match = route[k : k + 1] == expert
        named = named + jnp.where(match, 1.0, 0.0)
        gate = gate + jnp.where(match, gates[k : k + 1], 0.0)
    r0 = lax.broadcasted_iota(jnp.int32, (cols, cols), 0)
    r1 = lax.broadcasted_iota(jnp.int32, (cols, cols), 1)
    earlier = jnp.where((r0 < r1) & ((r0 < TOK) == (r1 < TOK)), 1.0, 0.0)
    position = nn(named.astype(BF), earlier.astype(BF))
    here = (position == (row % SLOT).astype(F32)) & (((row // SLOT) % 2 == 1) == (col >= TOK))
    return jnp.where(here, named, 0.0), jnp.where(here, gate, 0.0)


def select_body(where, own, other, sent, stage, sems):
    member_p, gate_p = tables(where, own[META:, :], other[META:, :], 0)
    copies = []
    for i in (0, 2, 1):
        member = member_p
        if i == 1:
            member, _ = tables(where, own[META:, :], other[META:, :], 1)
        at = slice(TOK * i, TOK * i + TOK)
        picked = nn(member.astype(BF), jnp.concatenate([own[at, :], other[at, :]], axis=0))
        if i == 2:
            picked = picked * jnp.sum(gate_p, axis=1, keepdims=True)
        at = slice(8 * i, 8 * i + 8)
        stage[:, at, :] = picked.astype(BF).reshape(PEERS, 8, 2 * Q)
        copies.append(pltpu.make_async_copy(stage.at[:, at, :], sent.at[:, at, :], sems.at[i]))
        copies[-1].start()
    for copy in copies:
        copy.wait()


def home_body(where, own, other, member_p, gates_f):
    meta_a, meta_b = own[META:, :], other[META:, :]
    member, _ = tables(where, meta_a, meta_b, 0)
    member_p[...] = member.T.astype(BF)
    _, gate = tables(where, meta_a, meta_b, 1)
    for n, piece in enumerate(pieces(gate.T)):
        gates_f[n] = piece


def preload_body(where, wg, wu, wd, ad, au, w, small, up, sems):
    e = where[2]
    moves = [(r.at[e], w.at[n]) for n, r in enumerate((wg, wu, wd))]
    moves += [(ad.at[e], small), (au.at[e], up)]
    run_all([pltpu.make_async_copy(a, b, sems.at[n]) for n, (a, b) in enumerate(moves)])


def arrive_body(where, w2, out, sems):
    run_all([pltpu.make_async_copy(w2, out, sems.at[0])])


def main_body(
    where, mine, theirs, own, small, up, w2, give, keep, inner, down_grad, down_grad2
):
    c = where[1]

    def weight(*kinds):
        def at(lanes):
            out = []
            for k in kinds:
                out += [up[:, lanes]] if k == 3 else [own[k, :, lanes], w2[192 * k : 192 * k + 192, lanes]]
            return jnp.concatenate(out, axis=0)

        return at

    def dot(i, w):
        total = None
        for ref, core in ((mine, c), (theirs, 1 - c)):
            for h in range(2):
                x = ref[:, 8 * i : 8 * i + 8, h * Q : (h + 1) * Q].reshape(ROWS, Q)
                part = nt(x, w(quarter(h, core)))
                total = part if total is None else total + part
        return total

    def expand(x, w, i):
        for out, core in ((give, 1 - c), (keep, c)):
            for h in range(2):
                total = nn(x, w(quarter(h, core))).astype(BF).reshape(PEERS, 8, Q)
                out[:, 8 * i : 8 * i + 8, h * Q : (h + 1) * Q] = total

    both, down, down_up = weight(0, 1), weight(2), weight(2, 3)
    pre = dot(1, both)
    gate_pre, up_pre = pre[:, :384], pre[:, 384:]
    expand((gate_pre * jax.nn.sigmoid(gate_pre) * up_pre).astype(BF), down, 1)
    tail = [w2[576:584, 256 * k : 256 * k + 192] for k in range(8)]
    adapters = jnp.concatenate([small[...], jnp.concatenate(tail, axis=0)], axis=1)
    pre = dot(0, both)
    gate_pre, up_pre = pre[:, :384], pre[:, 384:]
    sigmoid = jax.nn.sigmoid(gate_pre)
    activated = gate_pre * sigmoid
    hidden = (activated * up_pre).astype(BF)
    slope = up_pre * sigmoid * (1.0 + gate_pre * (1.0 - sigmoid))
    inner[...] = nt(hidden, adapters)
    pre = dot(2, down_up)
    inner_grad = (SCALE * pre[:, 384:]).astype(BF)
    grads = tn(inner_grad, hidden)
    down_grad[...] = grads[:, :192]
    down_grad2[...] = grads[:, 192:]
    hidden_grad = pre[:, :384] + nn(inner_grad, adapters)
    gate_grad = (hidden_grad * slope).astype(BF)
    up_grad = (hidden_grad * activated).astype(BF)
    expand(jnp.concatenate([gate_grad, up_grad], axis=1), both, 0)


def up_body(where, inner_a, inner_b, cot, out):
    inner = (inner_a[...] + inner_b[...]).astype(BF)
    out[...] = SCALE * tn(inner, cot[:, 16:24, :].reshape(ROWS, 2 * Q))


def combine_body(where, member, gates, back, own, to_xh, to_xl, to_both):
    for at, near, far in ((where[2], own, to_xl), (1 - where[2], to_xh, to_both)):
        lanes = pl.ds(pl.multiple_of(at * Q, Q), Q)
        grads = back[:, 0:8, lanes].reshape(ROWS, Q)
        frozen = back[:, 8:16, lanes].reshape(ROWS, Q)
        frozen = nn(gates[2], frozen) + nn(gates[1], frozen) + nn(gates[0], frozen)
        grads = nn(member[...], grads)
        for n, total in enumerate((frozen, grads)):
            near[n] = total[:TOK].astype(near.dtype)
            far[n] = total[TOK:].astype(far.dtype)


def swap(x, axis):
    return lax.ppermute(x, axis, [(0, 1), (1, 0)])


def swap_both(x):
    return lax.ppermute(x, ("xl", "xh"), [(i, 3 - i) for i in range(4)])


def exchange(x):
    return lax.all_to_all(x, ("y", "z"), split_axis=0, concat_axis=0, tiled=True)


def pick(c, a, b):
    return jnp.where(c == 0, a, b)


def step(
    policy_tokens, policy_cotangent, frozen_tokens, policy_route, policy_gates,
    frozen_route, frozen_gates, w_gate, w_up, w_down, adapter_down, adapter_up,
):
    c, xh = lax.axis_index("core"), lax.axis_index("xh")
    wg, wu = w_gate.swapaxes(1, 2), w_up.swapaxes(1, 2)
    ad = adapter_down.swapaxes(1, 2)
    own = kernel(
        halves_body, [sds((META + 8, 2 * Q), BF)],
        [policy_tokens, frozen_tokens, policy_cotangent,
         policy_route.T, policy_gates.T, frozen_route.T, frozen_gates.T],
        [pltpu.SemaphoreType.DMA((3, 2))], "hhhvvvv", "v", limit=FULL - 400000,
    )[0]
    other = swap(own, "xl")
    bundle = kernel(
        bundle_body, [sds((584, 4 * Q), BF)], [wg, wu, w_down, ad],
        [pltpu.VMEM((584, 4 * Q), BF), pltpu.VMEM((64, 192), BF), pltpu.SemaphoreType.DMA((2, 13))],
        "hhhh", "h", limit=FULL - 800000,
    )[0]
    w2 = swap(bundle, "xh")
    (sent,) = kernel(
        select_body, [sds((PEERS, 24, 2 * Q), BF)], [own, other],
        [pltpu.VMEM((PEERS, 24, 2 * Q), BF), pltpu.SemaphoreType.DMA((3,))], "vv", "h",
        limit=12 << 20,
    )
    member_p, gates_f = vmem_call(
        home_body, [sds((2 * TOK, ROWS), BF), sds((3, 2 * TOK, ROWS), BF)],
        [own, other], flops=10**8, mib=8,
    )
    mine = exchange(sent)
    theirs = swap(mine, "core")
    own_w, small, up = kernel(
        preload_body, [sds((3, 192, 4 * Q), BF), sds((64, 192), BF), sds((64, 4 * Q), BF)],
        [wg, wu, w_down, ad, adapter_up], [pltpu.SemaphoreType.DMA((5,))], "hhhhh", "vvv", limit=8 << 20,
    )
    (w2,) = kernel(
        arrive_body, [sds((584, 4 * Q), BF)], [w2], [pltpu.SemaphoreType.DMA((1,))],
        "h", "v", limit=8 << 20,
    )
    wide = sds((PEERS, 16, 2 * Q), BF)
    give, keep, inner, down_grad, down_grad2 = kernel(
        main_body,
        [wide, wide, sds((ROWS, 64), F32), sds((64, 192), F32), sds((64, 192), F32)],
        [mine, theirs, own_w, small, up, w2], [], "vvvvvv", "vvvvv", flops=4 * 10**9, limit=28 << 20,
    )
    total = (keep.astype(F32) + swap(give, "core").astype(F32)).astype(BF)
    back = exchange(total)
    own, to_xh, to_xl, to_both = vmem_call(
        combine_body, [sds((2, TOK, Q), F32)] + [sds((2, TOK, Q), BF)] * 3,
        [member_p, gates_f, back], flops=10**8, mib=8,
    )
    from_xh = swap(to_xh, "xh")
    from_xl = swap(to_xl, "xl")
    from_both = swap_both(to_both)
    outs = own + from_xh.astype(F32) + from_xl.astype(F32) + from_both.astype(F32)
    frozen_out, input_grad = outs[0].astype(BF), outs[1].astype(BF)

    (up_half,) = vmem_call(
        up_body, [sds((64, 2 * Q), F32)], [inner, swap(inner, "core"), mine],
        flops=10**8, mib=6,
    )
    up_other = swap(up_half, "core")
    lo, hi = pick(c, up_half, up_other), pick(c, up_other, up_half)
    up_own = jnp.concatenate([lo[:, :Q], hi[:, :Q], lo[:, Q:], hi[:, Q:]], axis=1)
    up_away = swap(up_own, "xh")
    up_grad = jnp.stack([pick(xh, up_own, up_away), pick(xh, up_away, up_own)])
    down_away = swap(down_grad2, "xh")
    down = jnp.stack([pick(xh, down_grad, down_away), pick(xh, down_away, down_grad)]).swapaxes(1, 2)
    return frozen_out, input_grad, down, up_grad


def solution(mesh):
    fine = Mesh(mesh.devices.reshape(4, 8, 2, 2, 2), ("y", "z", "xl", "xh", "core"))
    ex, pr = ("y", "z", "xl"), ("xh", "core")
    in_specs = (P(ex, None),) * 7 + (
        P(ex, None, pr), P(ex, None, pr), P(ex, pr, None), P(ex, pr, None), P(ex, None, None),
    )
    out_specs = (P(ex, pr), P(ex, pr), P(ex, pr, None), P(ex, None, None))
    return jax.shard_map(step, mesh=fine, in_specs=in_specs, out_specs=out_specs, check_vma=False)
```

```python
import jax
import jax.numpy as jnp
from jax import lax
from jax.experimental import pallas as pl
from jax.experimental.pallas import tpu as pltpu
from jax.sharding import Mesh, PartitionSpec as P

BF = jnp.bfloat16
F32 = jnp.float32
SCALE = 2.0
SLOT = 4
PEERS = 32
TOK = 48
Q = 512
ROWS = 256
META = 3 * TOK
FULL = 67043328


def nt(a, b):
    return lax.dot_general(a, b, (((1,), (1,)), ((), ())), preferred_element_type=F32)


def nn(a, b):
    return lax.dot_general(a, b, (((1,), (0,)), ((), ())), preferred_element_type=F32)


def tn(a, b):
    return lax.dot_general(a, b, (((0,), (0,)), ((), ())), preferred_element_type=F32)


def vmem_call(body, outs, args, flops=10**8, mib=16):
    return kernel(body, outs, args, [], "v" * len(args), "v" * len(outs), flops, mib << 20)


SPACES = {
    "h": pl.BlockSpec(memory_space=pltpu.HBM),
    "v": pl.BlockSpec(memory_space=pltpu.VMEM),
}


def kernel(body, outs, args, scratch, ins, places, flops=10**8, limit=FULL):
    moved = sum(a.size * a.dtype.itemsize for a in [*args, *outs])

    def run(*refs):
        xl, xh = lax.axis_index("xl"), lax.axis_index("xh")
        body((2 * xl + xh, lax.axis_index("core"), xh, xl), *refs)

    return pl.pallas_call(
        run,
        out_shape=outs,
        in_specs=[SPACES[x] for x in ins],
        out_specs=[SPACES[x] for x in places],
        scratch_shapes=scratch,
        compiler_params=pltpu.CompilerParams(vmem_limit_bytes=limit),
        cost_estimate=pl.CostEstimate(flops=flops, bytes_accessed=moved, transcendentals=0),
    )(*args)


def sds(shape, dtype):
    return jax.ShapeDtypeStruct(shape, dtype)


def quarter(h, core):
    return pl.ds(pl.multiple_of((2 * h + core) * Q, Q), Q)


def pieces(x):
    hi = x.astype(BF)
    rest = x - hi.astype(F32)
    mid = rest.astype(BF)
    return hi, mid, (rest - mid.astype(F32)).astype(BF)


def run_all(copies):
    for copy in copies:
        copy.start()
    for copy in copies:
        copy.wait()


def halves_body(where, policy, frozen, cotangent, route_p, gates_p, route_f, gates_f, own, sems):
    copies = []
    for n, ref in enumerate((policy, frozen, cotangent)):
        for h in range(2):
            copies.append(pltpu.make_async_copy(
                ref.at[:, quarter(h, where[1])],
                own.at[TOK * n : TOK * n + TOK, h * Q : (h + 1) * Q],
                sems.at[n, h],
            ))
    for copy in copies:
        copy.start()
    pad = jnp.zeros((8, 128 - TOK), BF)
    for n, (route, gates) in enumerate(((route_p, gates_p), (route_f, gates_f))):
        for p, x in enumerate((route[...].astype(F32).astype(BF), *pieces(gates[...]))):
            at = 128 * (4 * n + p)
            own[META:, at : at + 128] = jnp.concatenate([x, pad], axis=1)
    for copy in copies:
        copy.wait()


def bundle_body(where, wg, wu, wd, ad, out, stage, small, sems):
    away = 1 - where[2]
    last = pltpu.make_async_copy(ad.at[away], small, sems.at[0, 12])
    into, back = [], []
    for n, ref in enumerate((wg, wu, wd)):
        for k in range(4):
            at = 192 * n + 48 * k
            piece = stage.at[at : at + 48, :]
            src = ref.at[away, 48 * k : 48 * k + 48, :]
            into.append(pltpu.make_async_copy(src, piece, sems.at[0, 4 * n + k]))
            back.append(pltpu.make_async_copy(piece, out.at[at : at + 48, :], sems.at[1, 4 * n + k]))
    for copy in (*into, last):
        copy.start()
    for a, b in zip(into, back):
        a.wait()
        b.start()
    last.wait()
    pad = jnp.zeros((8, 64), BF)
    rest = [jnp.concatenate([small[8 * k : 8 * k + 8, :], pad], axis=1) for k in range(8)]
    stage[576:584, :] = jnp.concatenate(rest, axis=1)
    tail = pltpu.make_async_copy(stage.at[576:584, :], out.at[576:584, :], sems.at[1, 12])
    tail.start()
    for copy in (*back, tail):
        copy.wait()


def blocks(meta_a, meta_b, n):
    out = []
    for meta in (meta_a, meta_b):
        part = [meta[:, 128 * (4 * n + p) : 128 * (4 * n + p) + TOK].astype(F32) for p in range(4)]
        out.append((part[0], part[1] + part[2] + part[3]))
    return [jnp.concatenate([a, b], axis=1) for a, b in zip(*out)]


def tables(where, meta_a, meta_b, n):
    cols = 2 * TOK
    route, gates = blocks(meta_a, meta_b, n)
    col = lax.broadcasted_iota(jnp.int32, (ROWS, cols), 1)
    row = lax.broadcasted_iota(jnp.int32, (ROWS, cols), 0)
    expert = (4 * (row // 8) + where[0]).astype(F32)
    named = jnp.zeros((ROWS, cols), F32)
    gate = jnp.zeros((ROWS, cols), F32)
    for k in range(8):
        match = route[k : k + 1] == expert
        named = named + jnp.where(match, 1.0, 0.0)
        gate = gate + jnp.where(match, gates[k : k + 1], 0.0)
    r0 = lax.broadcasted_iota(jnp.int32, (cols, cols), 0)
    r1 = lax.broadcasted_iota(jnp.int32, (cols, cols), 1)
    earlier = jnp.where((r0 < r1) & ((r0 < TOK) == (r1 < TOK)), 1.0, 0.0)
    position = nn(named.astype(BF), earlier.astype(BF))
    here = (position == (row % SLOT).astype(F32)) & (((row // SLOT) % 2 == 1) == (col >= TOK))
    return jnp.where(here, named, 0.0), jnp.where(here, gate, 0.0)


def select_body(where, own, other, sent, stage, sems):
    member_p, gate_p = tables(where, own[META:, :], other[META:, :], 0)
    copies = []
    for i in (0, 2, 1):
        member = member_p
        if i == 1:
            member, _ = tables(where, own[META:, :], other[META:, :], 1)
        at = slice(TOK * i, TOK * i + TOK)
        picked = nn(member.astype(BF), jnp.concatenate([own[at, :], other[at, :]], axis=0))
        if i == 2:
            picked = picked * jnp.sum(gate_p, axis=1, keepdims=True)
        at = slice(8 * i, 8 * i + 8)
        stage[:, at, :] = picked.astype(BF).reshape(PEERS, 8, 2 * Q)
        copies.append(pltpu.make_async_copy(stage.at[:, at, :], sent.at[:, at, :], sems.at[i]))
        copies[-1].start()
    for copy in copies:
        copy.wait()


def home_body(where, own, out):
    rows = 2 * ROWS
    row = lax.broadcasted_iota(jnp.int32, (rows, TOK), 0)
    expert = (2 * (row // 8) + where[2]).astype(F32)
    r0 = lax.broadcasted_iota(jnp.int32, (TOK, TOK), 0)
    r1 = lax.broadcasted_iota(jnp.int32, (TOK, TOK), 1)
    earlier = jnp.where(r0 < r1, 1.0, 0.0).astype(BF)
    values = []
    for n in range(2):
        part = [own[META:, 128 * (4 * n + p) : 128 * (4 * n + p) + TOK].astype(F32) for p in range(4)]
        gates = part[1] + part[2] + part[3]
        named = jnp.zeros((rows, TOK), F32)
        value = jnp.zeros((rows, TOK), F32)
        for k in range(8):
            match = part[0][k : k + 1] == expert
            named = named + jnp.where(match, 1.0, 0.0)
            value = value + jnp.where(match, gates[k : k + 1] if n else 1.0, 0.0)
        position = nn(named.astype(BF), earlier)
        here = (position == (row % SLOT).astype(F32)) & ((row // SLOT) % 2 == n)
        values.append(jnp.where(here, value, 0.0).T)
    out[0] = values[0].astype(BF)
    for n, piece in enumerate(pieces(values[1])):
        out[1 + n] = piece


def preload_body(where, wg, wu, wd, ad, au, w, small, up, sems):
    e = where[2]
    moves = [(r.at[e], w.at[n]) for n, r in enumerate((wg, wu, wd))]
    moves += [(ad.at[e], small), (au.at[e], up)]
    run_all([pltpu.make_async_copy(a, b, sems.at[n]) for n, (a, b) in enumerate(moves)])


def arrive_body(where, w2, out, sems):
    run_all([pltpu.make_async_copy(w2, out, sems.at[0])])


def weights_of(own, w2, up=None):
    def weight(*kinds):
        def at(lanes):
            out = []
            for k in kinds:
                out += [up[:, lanes]] if k == 3 else [own[k, :, lanes], w2[192 * k : 192 * k + 192, lanes]]
            return jnp.concatenate(out, axis=0)

        return at

    return weight


def expand(where, core, frozen, frozen_w, grads, grads_w, out):
    first = lax.broadcasted_iota(jnp.int32, (ROWS, Q), 0) % 8 < SLOT
    xl = where[3]
    for h in range(2):
        at = quarter(h, core)
        a, b = nn(grads, grads_w(at)), nn(frozen, frozen_w(at))
        near = jnp.where(first, a, pltpu.roll(b, SLOT, 0))
        far = jnp.where(first, pltpu.roll(a, ROWS - SLOT, 0), b)
        for plane, total in ((xl, near), (1 - xl, far)):
            lanes = slice(h * Q, (h + 1) * Q)
            out[:, pl.ds(plane, 1), :, lanes] = total.astype(BF).reshape(PEERS, 1, 8, Q)


def keep_body(where, frozen, grads, own, w2, keep):
    weight = weights_of(own, w2)
    expand(where, where[1], frozen[...], weight(2), grads[...], weight(0, 1), keep)


def main_body(
    where, mine, theirs, own, small, up, w2, give, frozen, grads, inner, down_grad, down_grad2
):
    c = where[1]

    weight = weights_of(own, w2, up)

    def dot(i, w):
        total = None
        for ref, core in ((mine, c), (theirs, 1 - c)):
            for h in range(2):
                x = ref[:, 8 * i : 8 * i + 8, h * Q : (h + 1) * Q].reshape(ROWS, Q)
                part = nt(x, w(quarter(h, core)))
                total = part if total is None else total + part
        return total

    both, down, down_up = weight(0, 1), weight(2), weight(2, 3)
    pre = dot(1, both)
    gate_pre, up_pre = pre[:, :384], pre[:, 384:]
    frozen[...] = (gate_pre * jax.nn.sigmoid(gate_pre) * up_pre).astype(BF)
    tail = [w2[576:584, 256 * k : 256 * k + 192] for k in range(8)]
    adapters = jnp.concatenate([small[...], jnp.concatenate(tail, axis=0)], axis=1)
    pre = dot(0, both)
    gate_pre, up_pre = pre[:, :384], pre[:, 384:]
    sigmoid = jax.nn.sigmoid(gate_pre)
    activated = gate_pre * sigmoid
    hidden = (activated * up_pre).astype(BF)
    slope = up_pre * sigmoid * (1.0 + gate_pre * (1.0 - sigmoid))
    inner[...] = nt(hidden, adapters)
    pre = dot(2, down_up)
    inner_grad = (SCALE * pre[:, 384:]).astype(BF)
    adapter_grads = tn(inner_grad, hidden)
    down_grad[...] = adapter_grads[:, :192]
    down_grad2[...] = adapter_grads[:, 192:]
    hidden_grad = pre[:, :384] + nn(inner_grad, adapters)
    gate_grad = (hidden_grad * slope).astype(BF)
    up_grad = (hidden_grad * activated).astype(BF)
    both_grads = jnp.concatenate([gate_grad, up_grad], axis=1)
    grads[...] = both_grads
    expand(where, 1 - c, frozen[...], down, both_grads, both, give)


def finish_body(where, keep, got, out, stage, sems):
    copies = []
    for n in range(4):
        at = slice(8 * n, 8 * n + 8)
        stage[at] = (keep[at].astype(F32) + got[at].astype(F32)).astype(BF)
        copies.append(pltpu.make_async_copy(stage.at[at], out.at[at], sems.at[n]))
        copies[-1].start()
    for copy in copies:
        copy.wait()


def up_body(where, inner_a, inner_b, cot, out):
    inner = (inner_a[...] + inner_b[...]).astype(BF)
    out[...] = SCALE * tn(inner, cot[:, 16:24, :].reshape(ROWS, 2 * Q))


def combine_body(where, table, back, own, to_xh):
    for at, out in ((where[2], own), (1 - where[2], to_xh)):
        rows = back[:, :, pl.ds(pl.multiple_of(at * Q, Q), Q)].reshape(2 * ROWS, Q)
        out[0] = (nn(table[3], rows) + nn(table[2], rows) + nn(table[1], rows)).astype(out.dtype)
        out[1] = nn(table[0], rows).astype(out.dtype)


def swap(x, axis):
    return lax.ppermute(x, axis, [(0, 1), (1, 0)])


def exchange(x):
    return lax.all_to_all(x, ("y", "z"), split_axis=0, concat_axis=0, tiled=True)


def exchange_home(x):
    return lax.all_to_all(x, ("y", "z", "xl"), split_axis=0, concat_axis=0, tiled=True)


def pick(c, a, b):
    return jnp.where(c == 0, a, b)


def step(
    policy_tokens, policy_cotangent, frozen_tokens, policy_route, policy_gates,
    frozen_route, frozen_gates, w_gate, w_up, w_down, adapter_down, adapter_up,
):
    c, xh = lax.axis_index("core"), lax.axis_index("xh")
    wg, wu = w_gate.swapaxes(1, 2), w_up.swapaxes(1, 2)
    ad = adapter_down.swapaxes(1, 2)
    own = kernel(
        halves_body, [sds((META + 8, 2 * Q), BF)],
        [policy_tokens, frozen_tokens, policy_cotangent,
         policy_route.T, policy_gates.T, frozen_route.T, frozen_gates.T],
        [pltpu.SemaphoreType.DMA((3, 2))], "hhhvvvv", "v", limit=FULL - 400000,
    )[0]
    other = swap(own, "xl")
    bundle = kernel(
        bundle_body, [sds((584, 4 * Q), BF)], [wg, wu, w_down, ad],
        [pltpu.VMEM((584, 4 * Q), BF), pltpu.VMEM((64, 192), BF), pltpu.SemaphoreType.DMA((2, 13))],
        "hhhh", "h", limit=FULL - 800000,
    )[0]
    w2 = swap(bundle, "xh")
    (sent,) = kernel(
        select_body, [sds((PEERS, 24, 2 * Q), BF)], [own, other],
        [pltpu.VMEM((PEERS, 24, 2 * Q), BF), pltpu.SemaphoreType.DMA((3,))], "vv", "h",
        limit=12 << 20,
    )
    (table,) = vmem_call(home_body, [sds((4, TOK, 2 * ROWS), BF)], [own], mib=8)
    mine = exchange(sent)
    theirs = swap(mine, "core")
    own_w, small, up = kernel(
        preload_body, [sds((3, 192, 4 * Q), BF), sds((64, 192), BF), sds((64, 4 * Q), BF)],
        [wg, wu, w_down, ad, adapter_up], [pltpu.SemaphoreType.DMA((5,))], "hhhhh", "vvv", limit=8 << 20,
    )
    (w2,) = kernel(
        arrive_body, [sds((584, 4 * Q), BF)], [w2], [pltpu.SemaphoreType.DMA((1,))],
        "h", "v", limit=8 << 20,
    )
    wide = sds((PEERS, 2, 8, 2 * Q), BF)
    give, frozen, grads, inner, down_grad, down_grad2 = kernel(
        main_body,
        [wide, sds((ROWS, 384), BF), sds((ROWS, 768), BF),
         sds((ROWS, 64), F32), sds((64, 192), F32), sds((64, 192), F32)],
        [mine, theirs, own_w, small, up, w2], [], "vvvvvv", "vvvvvv", flops=4 * 10**9, limit=28 << 20,
    )
    got = swap(give, "core")
    (keep,) = kernel(keep_body, [wide], [frozen, grads, own_w, w2], [], "vvvv", "v", flops=10**9, limit=20 << 20)
    (total,) = kernel(
        finish_body, [wide], [keep, got],
        [pltpu.VMEM(wide.shape, BF), pltpu.SemaphoreType.DMA((4,))], "vv", "h", limit=48 << 20,
    )
    back = exchange_home(total.reshape(2 * PEERS, 8, 2 * Q))
    here, to_xh = vmem_call(combine_body, [sds((2, TOK, Q), F32), sds((2, TOK, Q), BF)], [table, back], mib=8)
    from_xh = swap(to_xh, "xh")
    outs = here + from_xh.astype(F32)
    frozen_out, input_grad = outs[0].astype(BF), outs[1].astype(BF)

    (up_half,) = vmem_call(
        up_body, [sds((64, 2 * Q), F32)], [inner, swap(inner, "core"), mine],
        flops=10**8, mib=6,
    )
    up_other = swap(up_half, "core")
    lo, hi = pick(c, up_half, up_other), pick(c, up_other, up_half)
    up_own = jnp.concatenate([lo[:, :Q], hi[:, :Q], lo[:, Q:], hi[:, Q:]], axis=1)
    up_away = swap(up_own, "xh")
    up_grad = jnp.stack([pick(xh, up_own, up_away), pick(xh, up_away, up_own)])
    down_away = swap(down_grad2, "xh")
    down = jnp.stack([pick(xh, down_grad, down_away), pick(xh, down_away, down_grad)]).swapaxes(1, 2)
    return frozen_out, input_grad, down, up_grad


def solution(mesh):
    fine = Mesh(mesh.devices.reshape(4, 8, 2, 2, 2), ("y", "z", "xl", "xh", "core"))
    ex, pr = ("y", "z", "xl"), ("xh", "core")
    in_specs = (P(ex, None),) * 7 + (
        P(ex, None, pr), P(ex, None, pr), P(ex, pr, None), P(ex, pr, None), P(ex, None, None),
    )
    out_specs = (P(ex, pr), P(ex, pr), P(ex, pr, None), P(ex, None, None))
    return jax.shard_map(step, mesh=fine, in_specs=in_specs, out_specs=out_specs, check_vma=False)
```

```python
import jax
import jax.numpy as jnp
from jax import lax
from jax.experimental import pallas as pl
from jax.experimental.pallas import tpu as pltpu
from jax.sharding import Mesh, PartitionSpec as P

BF = jnp.bfloat16
F32 = jnp.float32
SCALE = 2.0
SLOT = 4
PEERS = 32
TOK = 48
Q = 512
ROWS = 256
META = 3 * TOK
FULL = 67043328


def nt(a, b):
    return lax.dot_general(a, b, (((1,), (1,)), ((), ())), preferred_element_type=F32)


def nn(a, b):
    return lax.dot_general(a, b, (((1,), (0,)), ((), ())), preferred_element_type=F32)


def tn(a, b):
    return lax.dot_general(a, b, (((0,), (0,)), ((), ())), preferred_element_type=F32)


def vmem_call(body, outs, args, flops=10**8, mib=16):
    return kernel(body, outs, args, [], "v" * len(args), "v" * len(outs), flops, mib << 20)


SPACES = {
    "h": pl.BlockSpec(memory_space=pltpu.HBM),
    "v": pl.BlockSpec(memory_space=pltpu.VMEM),
}


def kernel(body, outs, args, scratch, ins, places, flops=10**8, limit=FULL):
    moved = sum(a.size * a.dtype.itemsize for a in [*args, *outs])

    def run(*refs):
        xl, xh = lax.axis_index("xl"), lax.axis_index("xh")
        body((2 * xl + xh, lax.axis_index("core"), xh, xl), *refs)

    return pl.pallas_call(
        run,
        out_shape=outs,
        in_specs=[SPACES[x] for x in ins],
        out_specs=[SPACES[x] for x in places],
        scratch_shapes=scratch,
        compiler_params=pltpu.CompilerParams(vmem_limit_bytes=limit),
        cost_estimate=pl.CostEstimate(flops=flops, bytes_accessed=moved, transcendentals=0),
    )(*args)


def sds(shape, dtype):
    return jax.ShapeDtypeStruct(shape, dtype)


def quarter(h, core):
    return pl.ds(pl.multiple_of((2 * h + core) * Q, Q), Q)


def pieces(x):
    hi = x.astype(BF)
    rest = x - hi.astype(F32)
    mid = rest.astype(BF)
    return hi, mid, (rest - mid.astype(F32)).astype(BF)


def run_all(copies):
    for copy in copies:
        copy.start()
    for copy in copies:
        copy.wait()


def halves_body(where, policy, frozen, cotangent, route_p, gates_p, route_f, gates_f, own, sems):
    copies = []
    for n, ref in enumerate((policy, frozen, cotangent)):
        for h in range(2):
            copies.append(pltpu.make_async_copy(
                ref.at[:, quarter(h, where[1])],
                own.at[TOK * n : TOK * n + TOK, h * Q : (h + 1) * Q],
                sems.at[n, h],
            ))
    for copy in copies:
        copy.start()
    pad = jnp.zeros((8, 128 - TOK), BF)
    for n, (route, gates) in enumerate(((route_p, gates_p), (route_f, gates_f))):
        for p, x in enumerate((route[...].astype(F32).astype(BF), *pieces(gates[...]))):
            at = 128 * (4 * n + p)
            own[META:, at : at + 128] = jnp.concatenate([x, pad], axis=1)
    for copy in copies:
        copy.wait()


def bundle_body(where, wg, wu, wd, ad, out, stage, small, sems):
    away = 1 - where[2]
    last = pltpu.make_async_copy(ad.at[away], small, sems.at[0, 12])
    into, back = [], []
    for n, ref in enumerate((wg, wu, wd)):
        for k in range(4):
            at = 192 * n + 48 * k
            piece = stage.at[at : at + 48, :]
            src = ref.at[away, 48 * k : 48 * k + 48, :]
            into.append(pltpu.make_async_copy(src, piece, sems.at[0, 4 * n + k]))
            back.append(pltpu.make_async_copy(piece, out.at[at : at + 48, :], sems.at[1, 4 * n + k]))
    for copy in (*into, last):
        copy.start()
    for a, b in zip(into, back):
        a.wait()
        b.start()
    last.wait()
    pad = jnp.zeros((8, 64), BF)
    rest = [jnp.concatenate([small[8 * k : 8 * k + 8, :], pad], axis=1) for k in range(8)]
    stage[576:584, :] = jnp.concatenate(rest, axis=1)
    tail = pltpu.make_async_copy(stage.at[576:584, :], out.at[576:584, :], sems.at[1, 12])
    tail.start()
    for copy in (*back, tail):
        copy.wait()


def blocks(meta_a, meta_b, n):
    out = []
    for meta in (meta_a, meta_b):
        part = [meta[:, 128 * (4 * n + p) : 128 * (4 * n + p) + TOK].astype(F32) for p in range(4)]
        out.append((part[0], part[1] + part[2] + part[3]))
    return [jnp.concatenate([a, b], axis=1) for a, b in zip(*out)]


def tables(where, meta_a, meta_b, n):
    cols = 2 * TOK
    route, gates = blocks(meta_a, meta_b, n)
    col = lax.broadcasted_iota(jnp.int32, (ROWS, cols), 1)
    row = lax.broadcasted_iota(jnp.int32, (ROWS, cols), 0)
    expert = (4 * (row // 8) + where[0]).astype(F32)
    named = jnp.zeros((ROWS, cols), F32)
    gate = jnp.zeros((ROWS, cols), F32)
    for k in range(8):
        match = route[k : k + 1] == expert
        named = named + jnp.where(match, 1.0, 0.0)
        gate = gate + jnp.where(match, gates[k : k + 1], 0.0)
    r0 = lax.broadcasted_iota(jnp.int32, (cols, cols), 0)
    r1 = lax.broadcasted_iota(jnp.int32, (cols, cols), 1)
    earlier = jnp.where((r0 < r1) & ((r0 < TOK) == (r1 < TOK)), 1.0, 0.0)
    position = nn(named.astype(BF), earlier.astype(BF))
    here = (position == (row % SLOT).astype(F32)) & (((row // SLOT) % 2 == 1) == (col >= TOK))
    return jnp.where(here, named, 0.0), jnp.where(here, gate, 0.0)


def select_body(where, own, other, sent, stage, sems):
    member_p, gate_p = tables(where, own[META:, :], other[META:, :], 0)
    copies = []
    for i in (0, 2, 1):
        member = member_p
        if i == 1:
            member, _ = tables(where, own[META:, :], other[META:, :], 1)
        at = slice(TOK * i, TOK * i + TOK)
        picked = nn(member.astype(BF), jnp.concatenate([own[at, :], other[at, :]], axis=0))
        if i == 2:
            picked = picked * jnp.sum(gate_p, axis=1, keepdims=True)
        at = slice(8 * i, 8 * i + 8)
        stage[:, at, :] = picked.astype(BF).reshape(PEERS, 8, 2 * Q)
        copies.append(pltpu.make_async_copy(stage.at[:, at, :], sent.at[:, at, :], sems.at[i]))
        copies[-1].start()
    for copy in copies:
        copy.wait()


def home_body(where, own, out):
    rows = 2 * ROWS
    row = lax.broadcasted_iota(jnp.int32, (rows, TOK), 0)
    expert = (2 * (row // 8) + where[2]).astype(F32)
    r0 = lax.broadcasted_iota(jnp.int32, (TOK, TOK), 0)
    r1 = lax.broadcasted_iota(jnp.int32, (TOK, TOK), 1)
    earlier = jnp.where(r0 < r1, 1.0, 0.0).astype(BF)
    values = []
    for n in range(2):
        part = [own[META:, 128 * (4 * n + p) : 128 * (4 * n + p) + TOK].astype(F32) for p in range(4)]
        gates = part[1] + part[2] + part[3]
        named = jnp.zeros((rows, TOK), F32)
        value = jnp.zeros((rows, TOK), F32)
        for k in range(8):
            match = part[0][k : k + 1] == expert
            named = named + jnp.where(match, 1.0, 0.0)
            value = value + jnp.where(match, gates[k : k + 1] if n else 1.0, 0.0)
        position = nn(named.astype(BF), earlier)
        here = (position == (row % SLOT).astype(F32)) & ((row // SLOT) % 2 == n)
        values.append(jnp.where(here, value, 0.0).T)
    out[0] = values[0].astype(BF)
    for n, piece in enumerate(pieces(values[1])):
        out[1 + n] = piece


def preload_body(where, wg, wu, wd, ad, au, w, small, up, sems):
    e = where[2]
    moves = [(r.at[e], w.at[n]) for n, r in enumerate((wg, wu, wd))]
    moves += [(ad.at[e], small), (au.at[e], up)]
    run_all([pltpu.make_async_copy(a, b, sems.at[n]) for n, (a, b) in enumerate(moves)])


def arrive_body(where, w2, out, sems):
    run_all([pltpu.make_async_copy(w2, out, sems.at[0])])


def weights_of(own, w2, up=None):
    def weight(*kinds):
        def at(lanes):
            out = []
            for k in kinds:
                out += [up[:, lanes]] if k == 3 else [own[k, :, lanes], w2[192 * k : 192 * k + 192, lanes]]
            return jnp.concatenate(out, axis=0)

        return at

    return weight


def expand(where, core, frozen, frozen_w, grads, grads_w, out):
    first = lax.broadcasted_iota(jnp.int32, (ROWS, Q), 0) % 8 < SLOT
    xl = where[3]
    for h in range(2):
        at = quarter(h, core)
        a, b = nn(grads, grads_w(at)), nn(frozen, frozen_w(at))
        near = jnp.where(first, a, pltpu.roll(b, SLOT, 0))
        far = jnp.where(first, pltpu.roll(a, ROWS - SLOT, 0), b)
        for plane, total in ((xl, near), (1 - xl, far)):
            lanes = slice(h * Q, (h + 1) * Q)
            out[:, pl.ds(plane, 1), :, lanes] = total.astype(BF).reshape(PEERS, 1, 8, Q)


def keep_body(where, frozen, grads, own, w2, keep):
    weight = weights_of(own, w2)
    expand(where, where[1], frozen[...], weight(2), grads[...], weight(0, 1), keep)


def main_body(
    where, mine, theirs, own, small, up, w2, give, frozen, grads, inner, down_grad, down_grad2
):
    c = where[1]

    weight = weights_of(own, w2, up)

    def dot(i, w):
        total = None
        for ref, core in ((mine, c), (theirs, 1 - c)):
            for h in range(2):
                x = ref[:, 8 * i : 8 * i + 8, h * Q : (h + 1) * Q].reshape(ROWS, Q)
                part = nt(x, w(quarter(h, core)))
                total = part if total is None else total + part
        return total

    both, down, down_up = weight(0, 1), weight(2), weight(2, 3)
    pre = dot(1, both)
    gate_pre, up_pre = pre[:, :384], pre[:, 384:]
    frozen[...] = (gate_pre * jax.nn.sigmoid(gate_pre) * up_pre).astype(BF)
    tail = [w2[576:584, 256 * k : 256 * k + 192] for k in range(8)]
    adapters = jnp.concatenate([small[...], jnp.concatenate(tail, axis=0)], axis=1)
    pre = dot(0, both)
    gate_pre, up_pre = pre[:, :384], pre[:, 384:]
    sigmoid = jax.nn.sigmoid(gate_pre)
    activated = gate_pre * sigmoid
    hidden = (activated * up_pre).astype(BF)
    slope = up_pre * sigmoid * (1.0 + gate_pre * (1.0 - sigmoid))
    inner[...] = nt(hidden, adapters)
    pre = dot(2, down_up)
    inner_grad = (SCALE * pre[:, 384:]).astype(BF)
    adapter_grads = tn(inner_grad, hidden)
    down_grad[...] = adapter_grads[:, :192]
    down_grad2[...] = adapter_grads[:, 192:]
    hidden_grad = pre[:, :384] + nn(inner_grad, adapters)
    gate_grad = (hidden_grad * slope).astype(BF)
    up_grad = (hidden_grad * activated).astype(BF)
    both_grads = jnp.concatenate([gate_grad, up_grad], axis=1)
    grads[...] = both_grads
    expand(where, 1 - c, frozen[...], down, both_grads, both, give)


def finish_body(where, keep, got, out, stage, sems):
    copies = []
    for n in range(4):
        at = slice(8 * n, 8 * n + 8)
        stage[at] = (keep[at].astype(F32) + got[at].astype(F32)).astype(BF)
        copies.append(pltpu.make_async_copy(stage.at[at], out.at[at], sems.at[n]))
        copies[-1].start()
    for copy in copies:
        copy.wait()


def last_body(where, here, there, frozen_out, input_grad):
    for n, out in enumerate((frozen_out, input_grad)):
        out[...] = (here[n] + there[n].astype(F32)).astype(BF)


def up_body(where, inner_a, inner_b, cot, out):
    inner = (inner_a[...] + inner_b[...]).astype(BF)
    out[...] = SCALE * tn(inner, cot[:, 16:24, :].reshape(ROWS, 2 * Q))


def combine_body(where, table, back, own, to_xh):
    for at, out in ((where[2], own), (1 - where[2], to_xh)):
        rows = back[:, :, pl.ds(pl.multiple_of(at * Q, Q), Q)].reshape(2 * ROWS, Q)
        out[0] = (nn(table[3], rows) + nn(table[2], rows) + nn(table[1], rows)).astype(out.dtype)
        out[1] = nn(table[0], rows).astype(out.dtype)


def swap(x, axis):
    return lax.ppermute(x, axis, [(0, 1), (1, 0)])


def exchange(x):
    return lax.all_to_all(x, ("y", "z"), split_axis=0, concat_axis=0, tiled=True)


def exchange_home(x):
    return lax.all_to_all(x, ("y", "z", "xl"), split_axis=0, concat_axis=0, tiled=True)


def pick(c, a, b):
    return jnp.where(c == 0, a, b)


def step(
    policy_tokens, policy_cotangent, frozen_tokens, policy_route, policy_gates,
    frozen_route, frozen_gates, w_gate, w_up, w_down, adapter_down, adapter_up,
):
    c, xh = lax.axis_index("core"), lax.axis_index("xh")
    wg, wu = w_gate.swapaxes(1, 2), w_up.swapaxes(1, 2)
    ad = adapter_down.swapaxes(1, 2)
    own = kernel(
        halves_body, [sds((META + 8, 2 * Q), BF)],
        [policy_tokens, frozen_tokens, policy_cotangent,
         policy_route.T, policy_gates.T, frozen_route.T, frozen_gates.T],
        [pltpu.SemaphoreType.DMA((3, 2))], "hhhvvvv", "v", limit=FULL - 400000,
    )[0]
    other = swap(own, "xl")
    bundle = kernel(
        bundle_body, [sds((584, 4 * Q), BF)], [wg, wu, w_down, ad],
        [pltpu.VMEM((584, 4 * Q), BF), pltpu.VMEM((64, 192), BF), pltpu.SemaphoreType.DMA((2, 13))],
        "hhhh", "h", limit=FULL - 800000,
    )[0]
    w2 = swap(bundle, "xh")
    (sent,) = kernel(
        select_body, [sds((PEERS, 24, 2 * Q), BF)], [own, other],
        [pltpu.VMEM((PEERS, 24, 2 * Q), BF), pltpu.SemaphoreType.DMA((3,))], "vv", "h",
        limit=12 << 20,
    )
    (table,) = vmem_call(home_body, [sds((4, TOK, 2 * ROWS), BF)], [own], mib=8)
    mine = exchange(sent)
    theirs = swap(mine, "core")
    own_w, small, up = kernel(
        preload_body, [sds((3, 192, 4 * Q), BF), sds((64, 192), BF), sds((64, 4 * Q), BF)],
        [wg, wu, w_down, ad, adapter_up], [pltpu.SemaphoreType.DMA((5,))], "hhhhh", "vvv", limit=8 << 20,
    )
    (w2,) = kernel(
        arrive_body, [sds((584, 4 * Q), BF)], [w2], [pltpu.SemaphoreType.DMA((1,))],
        "h", "v", limit=8 << 20,
    )
    wide = sds((PEERS, 2, 8, 2 * Q), BF)
    give, frozen, grads, inner, down_grad, down_grad2 = kernel(
        main_body,
        [wide, sds((ROWS, 384), BF), sds((ROWS, 768), BF),
         sds((ROWS, 64), F32), sds((64, 192), F32), sds((64, 192), F32)],
        [mine, theirs, own_w, small, up, w2], [], "vvvvvv", "vvvvvv", flops=4 * 10**9, limit=28 << 20,
    )
    got = swap(give, "core")
    (keep,) = kernel(keep_body, [wide], [frozen, grads, own_w, w2], [], "vvvv", "v", flops=10**9, limit=20 << 20)
    (total,) = kernel(
        finish_body, [wide], [keep, got],
        [pltpu.VMEM(wide.shape, BF), pltpu.SemaphoreType.DMA((4,))], "vv", "h", limit=48 << 20,
    )
    back = exchange_home(total.reshape(2 * PEERS, 8, 2 * Q))
    here, to_xh = vmem_call(combine_body, [sds((2, TOK, Q), F32), sds((2, TOK, Q), BF)], [table, back], mib=8)
    from_xh = swap(to_xh, "xh")
    frozen_out, input_grad = vmem_call(last_body, [sds((TOK, Q), BF)] * 2, [here, from_xh], mib=4)

    (up_half,) = vmem_call(
        up_body, [sds((64, 2 * Q), F32)], [inner, swap(inner, "core"), mine],
        flops=10**8, mib=6,
    )
    up_other = swap(up_half, "core")
    lo, hi = pick(c, up_half, up_other), pick(c, up_other, up_half)
    up_own = jnp.concatenate([lo[:, :Q], hi[:, :Q], lo[:, Q:], hi[:, Q:]], axis=1)
    up_away = swap(up_own, "xh")
    up_grad = jnp.stack([pick(xh, up_own, up_away), pick(xh, up_away, up_own)])
    down_away = swap(down_grad2, "xh")
    down = jnp.stack([pick(xh, down_grad, down_away), pick(xh, down_away, down_grad)]).swapaxes(1, 2)
    return frozen_out, input_grad, down, up_grad


def solution(mesh):
    fine = Mesh(mesh.devices.reshape(4, 8, 2, 2, 2), ("y", "z", "xl", "xh", "core"))
    ex, pr = ("y", "z", "xl"), ("xh", "core")
    in_specs = (P(ex, None),) * 7 + (
        P(ex, None, pr), P(ex, None, pr), P(ex, pr, None), P(ex, pr, None), P(ex, None, None),
    )
    out_specs = (P(ex, pr), P(ex, pr), P(ex, pr, None), P(ex, None, None))
    return jax.shard_map(step, mesh=fine, in_specs=in_specs, out_specs=out_specs, check_vma=False)
```

```python
import functools
import jax
import jax.numpy as jnp
from jax import lax
from jax.experimental import pallas as pl
from jax.experimental.pallas import tpu as pltpu
from jax.sharding import Mesh, PartitionSpec as P

BF = jnp.bfloat16
F32 = jnp.float32
SCALE = 2.0
SLOT = 4
PEERS = 32
TOK = 48
Q = 512
ROWS = 256
META = 3 * TOK
FULL = 67043328


def nt(a, b):
    return lax.dot_general(a, b, (((1,), (1,)), ((), ())), preferred_element_type=F32)


def nn(a, b):
    return lax.dot_general(a, b, (((1,), (0,)), ((), ())), preferred_element_type=F32)


def tn(a, b):
    return lax.dot_general(a, b, (((0,), (0,)), ((), ())), preferred_element_type=F32)


def vmem_call(body, outs, args, flops=10**8, mib=16):
    return kernel(body, outs, args, [], "v" * len(args), "v" * len(outs), flops, mib << 20)


SPACES = {
    "h": pl.BlockSpec(memory_space=pltpu.HBM),
    "v": pl.BlockSpec(memory_space=pltpu.VMEM),
}


def kernel(body, outs, args, scratch, ins, places, flops=10**8, limit=FULL):
    moved = sum(a.size * a.dtype.itemsize for a in [*args, *outs])

    def run(*refs):
        xl, xh = lax.axis_index("xl"), lax.axis_index("xh")
        body((2 * xl + xh, lax.axis_index("core"), xh, xl), *refs)

    return pl.pallas_call(
        run,
        out_shape=outs,
        in_specs=[SPACES[x] for x in ins],
        out_specs=[SPACES[x] for x in places],
        scratch_shapes=scratch,
        compiler_params=pltpu.CompilerParams(vmem_limit_bytes=limit),
        cost_estimate=pl.CostEstimate(flops=flops, bytes_accessed=moved, transcendentals=0),
    )(*args)


def sds(shape, dtype):
    return jax.ShapeDtypeStruct(shape, dtype)


def quarter(h, core):
    return pl.ds(pl.multiple_of((2 * h + core) * Q, Q), Q)


def pieces(x):
    hi = x.astype(BF)
    rest = x - hi.astype(F32)
    mid = rest.astype(BF)
    return hi, mid, (rest - mid.astype(F32)).astype(BF)


def run_all(copies):
    for copy in copies:
        copy.start()
    for copy in copies:
        copy.wait()


def halves_body(where, policy, frozen, cotangent, route_p, gates_p, route_f, gates_f, own, sems):
    copies = []
    for n, ref in enumerate((policy, frozen, cotangent)):
        for h in range(2):
            copies.append(pltpu.make_async_copy(
                ref.at[:, quarter(h, where[1])],
                own.at[TOK * n : TOK * n + TOK, h * Q : (h + 1) * Q],
                sems.at[n, h],
            ))
    for copy in copies:
        copy.start()
    pad = jnp.zeros((8, 128 - TOK), BF)
    for n, (route, gates) in enumerate(((route_p, gates_p), (route_f, gates_f))):
        for p, x in enumerate((route[...].astype(F32).astype(BF), *pieces(gates[...]))):
            at = 128 * (4 * n + p)
            own[META:, at : at + 128] = jnp.concatenate([x, pad], axis=1)
    for copy in copies:
        copy.wait()


def bundle_body(where, wg, wu, wd, ad, out, stage, small, sems):
    away = 1 - where[2]
    last = pltpu.make_async_copy(ad.at[away], small, sems.at[0, 12])
    into, back = [], []
    for n, ref in enumerate((wg, wu, wd)):
        for k in range(4):
            at = 192 * n + 48 * k
            piece = stage.at[at : at + 48, :]
            src = ref.at[away, 48 * k : 48 * k + 48, :]
            into.append(pltpu.make_async_copy(src, piece, sems.at[0, 4 * n + k]))
            back.append(pltpu.make_async_copy(piece, out.at[at : at + 48, :], sems.at[1, 4 * n + k]))
    for copy in (*into, last):
        copy.start()
    for a, b in zip(into, back):
        a.wait()
        b.start()
    last.wait()
    pad = jnp.zeros((8, 64), BF)
    rest = [jnp.concatenate([small[8 * k : 8 * k + 8, :], pad], axis=1) for k in range(8)]
    stage[576:584, :] = jnp.concatenate(rest, axis=1)
    tail = pltpu.make_async_copy(stage.at[576:584, :], out.at[576:584, :], sems.at[1, 12])
    tail.start()
    for copy in (*back, tail):
        copy.wait()


def blocks(meta_a, meta_b, n):
    out = []
    for meta in (meta_a, meta_b):
        part = [meta[:, 128 * (4 * n + p) : 128 * (4 * n + p) + TOK].astype(F32) for p in range(4)]
        out.append((part[0], part[1] + part[2] + part[3]))
    return [jnp.concatenate([a, b], axis=1) for a, b in zip(*out)]


def tables(where, meta_a, meta_b, n):
    cols = 2 * TOK
    route, gates = blocks(meta_a, meta_b, n)
    col = lax.broadcasted_iota(jnp.int32, (ROWS, cols), 1)
    row = lax.broadcasted_iota(jnp.int32, (ROWS, cols), 0)
    expert = (4 * (row // 8) + where[0]).astype(F32)
    named = jnp.zeros((ROWS, cols), F32)
    gate = jnp.zeros((ROWS, cols), F32)
    for k in range(8):
        match = route[k : k + 1] == expert
        named = named + jnp.where(match, 1.0, 0.0)
        gate = gate + jnp.where(match, gates[k : k + 1], 0.0)
    r0 = lax.broadcasted_iota(jnp.int32, (cols, cols), 0)
    r1 = lax.broadcasted_iota(jnp.int32, (cols, cols), 1)
    earlier = jnp.where((r0 < r1) & ((r0 < TOK) == (r1 < TOK)), 1.0, 0.0)
    position = nn(named.astype(BF), earlier.astype(BF))
    here = (position == (row % SLOT).astype(F32)) & (((row // SLOT) % 2 == 1) == (col >= TOK))
    return jnp.where(here, named, 0.0), jnp.where(here, gate, 0.0)


def select_body(where, own, other, sent, stage, sems):
    member_p, gate_p = tables(where, own[META:, :], other[META:, :], 0)
    copies = []
    for i in (0, 2, 1):
        member = member_p
        if i == 1:
            member, _ = tables(where, own[META:, :], other[META:, :], 1)
        at = slice(TOK * i, TOK * i + TOK)
        picked = nn(member.astype(BF), jnp.concatenate([own[at, :], other[at, :]], axis=0))
        if i == 2:
            picked = picked * jnp.sum(gate_p, axis=1, keepdims=True)
        at = slice(8 * i, 8 * i + 8)
        stage[:, at, :] = picked.astype(BF).reshape(PEERS, 8, 2 * Q)
        copies.append(pltpu.make_async_copy(stage.at[:, at, :], sent.at[:, at, :], sems.at[i]))
        copies[-1].start()
    for copy in copies:
        copy.wait()


def home_body(where, own, out):
    rows = 2 * ROWS
    row = lax.broadcasted_iota(jnp.int32, (rows, TOK), 0)
    expert = (2 * (row // 8) + where[2]).astype(F32)
    r0 = lax.broadcasted_iota(jnp.int32, (TOK, TOK), 0)
    r1 = lax.broadcasted_iota(jnp.int32, (TOK, TOK), 1)
    earlier = jnp.where(r0 < r1, 1.0, 0.0).astype(BF)
    values = []
    for n in range(2):
        part = [own[META:, 128 * (4 * n + p) : 128 * (4 * n + p) + TOK].astype(F32) for p in range(4)]
        gates = part[1] + part[2] + part[3]
        named = jnp.zeros((rows, TOK), F32)
        value = jnp.zeros((rows, TOK), F32)
        for k in range(8):
            match = part[0][k : k + 1] == expert
            named = named + jnp.where(match, 1.0, 0.0)
            value = value + jnp.where(match, gates[k : k + 1] if n else 1.0, 0.0)
        position = nn(named.astype(BF), earlier)
        here = (position == (row % SLOT).astype(F32)) & ((row // SLOT) % 2 == n)
        values.append(jnp.where(here, value, 0.0).T)
    out[0] = values[0].astype(BF)
    for n, piece in enumerate(pieces(values[1])):
        out[1 + n] = piece


def preload_body(where, wg, wu, wd, ad, au, w, small, up, sems):
    e = where[2]
    moves = [(r.at[e], w.at[n]) for n, r in enumerate((wg, wu, wd))]
    moves += [(ad.at[e], small), (au.at[e], up)]
    run_all([pltpu.make_async_copy(a, b, sems.at[n]) for n, (a, b) in enumerate(moves)])


def arrive_body(where, w2, out, sems):
    run_all([pltpu.make_async_copy(w2, out, sems.at[0])])


def weights_of(own, w2, up=None):
    def weight(*kinds):
        def at(lanes):
            out = []
            for k in kinds:
                out += [up[:, lanes]] if k == 3 else [own[k, :, lanes], w2[192 * k : 192 * k + 192, lanes]]
            return jnp.concatenate(out, axis=0)

        return at

    return weight


def expand(where, core, frozen, frozen_w, grads, grads_w, out):
    first = lax.broadcasted_iota(jnp.int32, (ROWS, Q), 0) % 8 < SLOT
    xl = where[3]
    for h in range(2):
        at = quarter(h, core)
        a, b = nn(grads, grads_w(at)), nn(frozen, frozen_w(at))
        near = jnp.where(first, a, pltpu.roll(b, SLOT, 0))
        far = jnp.where(first, pltpu.roll(a, ROWS - SLOT, 0), b)
        for plane, total in ((xl, near), (1 - xl, far)):
            lanes = slice(h * Q, (h + 1) * Q)
            out[:, pl.ds(plane, 1), :, lanes] = total.astype(BF).reshape(PEERS, 1, 8, Q)


def keep_body(where, frozen, grads, own, w2, keep):
    weight = weights_of(own, w2)
    expand(where, where[1], frozen[...], weight(2), grads[...], weight(0, 1), keep)


def main_body(
    where, mine, theirs, own, small, up, w2, give, frozen, grads, inner, down_grad, down_grad2
):
    c = where[1]

    weight = weights_of(own, w2, up)

    def dot(i, w):
        total = None
        for ref, core in ((mine, c), (theirs, 1 - c)):
            for h in range(2):
                x = ref[:, 8 * i : 8 * i + 8, h * Q : (h + 1) * Q].reshape(ROWS, Q)
                part = nt(x, w(quarter(h, core)))
                total = part if total is None else total + part
        return total

    both, down, down_up = weight(0, 1), weight(2), weight(2, 3)
    pre = dot(1, both)
    gate_pre, up_pre = pre[:, :384], pre[:, 384:]
    frozen[...] = (gate_pre * jax.nn.sigmoid(gate_pre) * up_pre).astype(BF)
    tail = [w2[576:584, 256 * k : 256 * k + 192] for k in range(8)]
    adapters = jnp.concatenate([small[...], jnp.concatenate(tail, axis=0)], axis=1)
    pre = dot(0, both)
    gate_pre, up_pre = pre[:, :384], pre[:, 384:]
    sigmoid = jax.nn.sigmoid(gate_pre)
    activated = gate_pre * sigmoid
    hidden = (activated * up_pre).astype(BF)
    slope = up_pre * sigmoid * (1.0 + gate_pre * (1.0 - sigmoid))
    inner[...] = nt(hidden, adapters)
    pre = dot(2, down_up)
    inner_grad = (SCALE * pre[:, 384:]).astype(BF)
    adapter_grads = tn(inner_grad, hidden)
    down_grad[...] = adapter_grads[:, :192]
    down_grad2[...] = adapter_grads[:, 192:]
    hidden_grad = pre[:, :384] + nn(inner_grad, adapters)
    gate_grad = (hidden_grad * slope).astype(BF)
    up_grad = (hidden_grad * activated).astype(BF)
    both_grads = jnp.concatenate([gate_grad, up_grad], axis=1)
    grads[...] = both_grads
    expand(where, 1 - c, frozen[...], down, both_grads, both, give)


def finish_body(where, keep, got, out, stage, sems):
    copies = []
    for n in range(4):
        at = slice(8 * n, 8 * n + 8)
        stage[at] = (keep[at].astype(F32) + got[at].astype(F32)).astype(BF)
        copies.append(pltpu.make_async_copy(stage.at[at], out.at[at], sems.at[n]))
        copies[-1].start()
    for copy in copies:
        copy.wait()


def last_body(where, here, there, frozen_out, input_grad):
    for n, out in enumerate((frozen_out, input_grad)):
        out[...] = (here[n] + there[n].astype(F32)).astype(BF)


def up_body(where, inner_a, inner_b, cot, out):
    inner = (inner_a[...] + inner_b[...]).astype(BF)
    out[...] = SCALE * tn(inner, cot[:, 16:24, :].reshape(ROWS, 2 * Q))


def combine_body(away, where, table, back, out):
    at = 1 - where[2] if away else where[2]
    rows = back[:, :, pl.ds(pl.multiple_of(at * Q, Q), Q)].reshape(2 * ROWS, Q)
    out[0] = (nn(table[3], rows) + nn(table[2], rows) + nn(table[1], rows)).astype(out.dtype)
    out[1] = nn(table[0], rows).astype(out.dtype)


def swap(x, axis):
    return lax.ppermute(x, axis, [(0, 1), (1, 0)])


def exchange(x):
    return lax.all_to_all(x, ("y", "z"), split_axis=0, concat_axis=0, tiled=True)


def exchange_home(x):
    return lax.all_to_all(x, ("y", "z", "xl"), split_axis=0, concat_axis=0, tiled=True)


def pick(c, a, b):
    return jnp.where(c == 0, a, b)


def step(
    policy_tokens, policy_cotangent, frozen_tokens, policy_route, policy_gates,
    frozen_route, frozen_gates, w_gate, w_up, w_down, adapter_down, adapter_up,
):
    c, xh = lax.axis_index("core"), lax.axis_index("xh")
    wg, wu = w_gate.swapaxes(1, 2), w_up.swapaxes(1, 2)
    ad = adapter_down.swapaxes(1, 2)
    own = kernel(
        halves_body, [sds((META + 8, 2 * Q), BF)],
        [policy_tokens, frozen_tokens, policy_cotangent,
         policy_route.T, policy_gates.T, frozen_route.T, frozen_gates.T],
        [pltpu.SemaphoreType.DMA((3, 2))], "hhhvvvv", "v", limit=FULL - 400000,
    )[0]
    other = swap(own, "xl")
    bundle = kernel(
        bundle_body, [sds((584, 4 * Q), BF)], [wg, wu, w_down, ad],
        [pltpu.VMEM((584, 4 * Q), BF), pltpu.VMEM((64, 192), BF), pltpu.SemaphoreType.DMA((2, 13))],
        "hhhh", "h", limit=FULL - 800000,
    )[0]
    w2 = swap(bundle, "xh")
    (sent,) = kernel(
        select_body, [sds((PEERS, 24, 2 * Q), BF)], [own, other],
        [pltpu.VMEM((PEERS, 24, 2 * Q), BF), pltpu.SemaphoreType.DMA((3,))], "vv", "h",
        limit=12 << 20,
    )
    (table,) = vmem_call(home_body, [sds((4, TOK, 2 * ROWS), BF)], [own], mib=8)
    mine = exchange(sent)
    theirs = swap(mine, "core")
    own_w, small, up = kernel(
        preload_body, [sds((3, 192, 4 * Q), BF), sds((64, 192), BF), sds((64, 4 * Q), BF)],
        [wg, wu, w_down, ad, adapter_up], [pltpu.SemaphoreType.DMA((5,))], "hhhhh", "vvv", limit=8 << 20,
    )
    (w2,) = kernel(
        arrive_body, [sds((584, 4 * Q), BF)], [w2], [pltpu.SemaphoreType.DMA((1,))],
        "h", "v", limit=8 << 20,
    )
    wide = sds((PEERS, 2, 8, 2 * Q), BF)
    give, frozen, grads, inner, down_grad, down_grad2 = kernel(
        main_body,
        [wide, sds((ROWS, 384), BF), sds((ROWS, 768), BF),
         sds((ROWS, 64), F32), sds((64, 192), F32), sds((64, 192), F32)],
        [mine, theirs, own_w, small, up, w2], [], "vvvvvv", "vvvvvv", flops=4 * 10**9, limit=28 << 20,
    )
    got = swap(give, "core")
    (keep,) = kernel(keep_body, [wide], [frozen, grads, own_w, w2], [], "vvvv", "v", flops=10**9, limit=20 << 20)
    (total,) = kernel(
        finish_body, [wide], [keep, got],
        [pltpu.VMEM(wide.shape, BF), pltpu.SemaphoreType.DMA((4,))], "vv", "h", limit=48 << 20,
    )
    back = exchange_home(total.reshape(2 * PEERS, 8, 2 * Q))
    (to_xh,) = vmem_call(functools.partial(combine_body, True), [sds((2, TOK, Q), BF)], [table, back], mib=8)
    (here,) = vmem_call(functools.partial(combine_body, False), [sds((2, TOK, Q), F32)], [table, back], mib=8)
    from_xh = swap(to_xh, "xh")
    frozen_out, input_grad = vmem_call(last_body, [sds((TOK, Q), BF)] * 2, [here, from_xh], mib=4)

    (up_half,) = vmem_call(
        up_body, [sds((64, 2 * Q), F32)], [inner, swap(inner, "core"), mine],
        flops=10**8, mib=6,
    )
    up_other = swap(up_half, "core")
    lo, hi = pick(c, up_half, up_other), pick(c, up_other, up_half)
    up_own = jnp.concatenate([lo[:, :Q], hi[:, :Q], lo[:, Q:], hi[:, Q:]], axis=1)
    up_away = swap(up_own, "xh")
    up_grad = jnp.stack([pick(xh, up_own, up_away), pick(xh, up_away, up_own)])
    down_away = swap(down_grad2, "xh")
    down = jnp.stack([pick(xh, down_grad, down_away), pick(xh, down_away, down_grad)]).swapaxes(1, 2)
    return frozen_out, input_grad, down, up_grad


def solution(mesh):
    fine = Mesh(mesh.devices.reshape(4, 8, 2, 2, 2), ("y", "z", "xl", "xh", "core"))
    ex, pr = ("y", "z", "xl"), ("xh", "core")
    in_specs = (P(ex, None),) * 7 + (
        P(ex, None, pr), P(ex, None, pr), P(ex, pr, None), P(ex, pr, None), P(ex, None, None),
    )
    out_specs = (P(ex, pr), P(ex, pr), P(ex, pr, None), P(ex, None, None))
    return jax.shard_map(step, mesh=fine, in_specs=in_specs, out_specs=out_specs, check_vma=False)
```
